256 devices in a mesh: sub: 8 (over x, core), lat: 8 (over z_lo, y), lon: 4 (over z_hi).
Axes of the slice: x: 4, y: 4, z: 8 (z_hi: 4, z_lo: 2; z = z_hi * 2 + z_lo), core: 2. Of those that a mesh axis runs over, the one named last changes fastest.
Arguments:
- segment_launch_values: float32 [8, 3, 4096, 1024], P('sub', None, 'lat', 'lon'), may hold values from -1.8 to 1.8
- initial_backdrop: float32 [3, 4096, 1024], P(None, 'lat', 'lon'), may hold values from -1.8 to 1.8
- spectral_inverse_variances: float32 [3, 513], replicated, may hold values from 0.3 to 3
Outputs:
- weighted_defects: float32 [8, 3, 4096, 1024], P('sub', None, 'lat', 'lon')
The draws below stay inside these ranges and needn't reach their ends.
All inputs are finite; a program needn't handle non-finite values.
Results may differ from the reference program's by a relative error of at most 0.00017.
Values sent between devices are 32-bit elements; how exact they have to be, the bound alone decides.
No kernel may reach another device: no remote copies, remote signals or barrier semaphores. Data moves between devices by JAX's collectives and lax.ppermute only.
A program may use at most 64 MiB of HBM per device.

```python
import math
import jax
import jax.numpy as jnp
from jax import lax

NLON = 1024
STEPS = 3
NLAT = 4096
NSUB = 8
ZONAL_MODES = 513


def level_of(own_key, dims, shards, least, high):
    def one(axis_at, shards_of):
        draws = jax.random.uniform(jax.random.fold_in(jax.random.fold_in(own_key, 6), axis_at), (shards_of,), jnp.float32, least / len(shards), high / len(shards))
        return jnp.repeat(jnp.exp(draws), dims[axis_at] // shards_of).reshape((-1,) + (1,) * (len(dims) - axis_at - 1))

    factor_of = one(*shards[0])
    for cut in shards[1:]:
        factor_of = factor_of * one(*cut)
    return factor_of


def centred(key, extent, width, limit, shards=(), dtype=jnp.bfloat16):
    values = width * jax.random.normal(key, extent, jnp.float32)
    if shards:
        values = values * level_of(key, extent, shards, -0.22, 0.18)
    return jnp.clip(values, -limit, limit).astype(dtype)


def setup_inputs(seed: int = 0) -> dict:
    key_of = jax.random.split(jax.random.key(seed), 4)
    return {
        "segment_launch_values": centred(key_of[0], (NSUB, 3, NLAT, NLON), 0.3, 1.8, ((0, 8), (2, 8), (3, 4)), jnp.float32),
        "initial_backdrop": centred(key_of[1], (3, NLAT, NLON), 0.3, 1.8, ((1, 8), (2, 4)), jnp.float32),
        "spectral_inverse_variances": jnp.clip(jnp.exp(jax.random.uniform(key_of[2], (3, ZONAL_MODES), jnp.float32, math.log(0.3), math.log(3.0))), 0.3, 3.0),
    }


time_step = 0.5
coriolis_peak = 0.4


def latitude_tendencies(total_rows, first_row, count):
    index = (first_row + jnp.arange(count)).astype(jnp.float32)
    return (coriolis_peak * jnp.sin(2.0 * jnp.pi * (index + 0.5) / total_rows))[:, None]


def centre(field):
    return field[1:-1, 1:-1]


def along_lon(field):
    return 0.5 * (field[1:-1, 2:] - field[1:-1, :-2])


def along_lat(field):
    return 0.5 * (field[2:, 1:-1] - field[:-2, 1:-1])


def tendency(padded, coriolis):
    height = padded[0]
    zonal = padded[1]
    meridional = padded[2]
    depth = 1.0 + height
    height_rate = -(along_lon(depth * zonal) + along_lat(depth * meridional))
    zonal_mid = centre(zonal)
    merid_mid = centre(meridional)
    zonal_rate = -(zonal_mid * along_lon(zonal) + merid_mid * along_lat(zonal)) + coriolis * merid_mid - along_lon(height)
    merid_rate = -(zonal_mid * along_lon(meridional) + merid_mid * along_lat(meridional)) - coriolis * zonal_mid - along_lat(height)
    return jnp.stack([height_rate, zonal_rate, merid_rate])


def wrapped_rate(flow_variables, coriolis):
    padded = jnp.pad(flow_variables, ((0, 0), (1, 1), (1, 1)), mode="wrap")
    return tendency(padded, coriolis)


def model_step(flow_variables, coriolis):
    first = flow_variables + time_step * wrapped_rate(flow_variables, coriolis)
    second = 0.75 * flow_variables + 0.25 * (first + time_step * wrapped_rate(first, coriolis))
    return (1.0 / 3.0) * flow_variables + (2.0 / 3.0) * (second + time_step * wrapped_rate(second, coriolis))


def reference(segment_launch_values, initial_backdrop, spectral_inverse_variances):
    coriolis = latitude_tendencies(NLAT, 0, NLAT)

    def propagated_estimate(flow_variables):
        for step_number in range(STEPS):
            flow_variables = model_step(flow_variables, coriolis)
        return flow_variables

    interval_predictions = lax.map(propagated_estimate, segment_launch_values)
    preceding_interval = jnp.concatenate([initial_backdrop[None], interval_predictions[:-1]], axis=0)
    mismatch_misfits = segment_launch_values - preceding_interval
    spectral_coefficients = jnp.fft.rfft(mismatch_misfits, axis=-1) * spectral_inverse_variances[None, :, None, :]
    return jnp.fft.irfft(spectral_coefficients, n=NLON, axis=-1).astype(jnp.float32)
```

```python
import functools

import numpy as np
import jax
import jax.numpy as jnp
from jax import lax
from jax.experimental import pallas as pl
from jax.experimental.pallas import tpu as pltpu
from jax.sharding import PartitionSpec as P

NLON = 1024
STEPS = 3
time_step = 0.5
coriolis_peak = 0.4

SUB = 8
LON = 4
ROWS = 128
HALO = 3 * STEPS
FIRST = 96
MID = 16
HALF = 64
GROUP = 4
F32 = jnp.float32
BF16 = jnp.bfloat16


def unpack_rows(dst, piece, field, first, count, row0, block):
    for r in range(0, count, 8):
        for half in range(2):
            dst[field, pl.ds((row0 + r) * 8 + 2 * block + half, 8, stride=8), :] = piece[
                first + r : first + r + 8, 128 * half : 128 * half + 128
            ]


def stage(src, base, dst, f_ref, lo, rows, kind):
    lane = lax.broadcasted_iota(jnp.int32, (8, 128), 1)
    is_first = lane == 0
    is_last = lane == 127

    def dx(a):
        up = pltpu.roll(a, 127, 1)
        down = pltpu.roll(a, 1, 1)
        up = jnp.where(is_last, pltpu.roll(up, 7, 0), up)
        down = jnp.where(is_first, pltpu.roll(down, 1, 0), down)
        return up - down

    def body(g, carry):
        row = lo + g * GROUP

        def load(ref, c, k):
            return ref[c, pl.ds(pl.multiple_of((row + k) * 8, 8), 8), :]

        h = [load(src, 0, k) for k in range(-1, GROUP + 1)]
        u = [load(src, 1, k) for k in range(-1, GROUP + 1)]
        v = [load(src, 2, k) for k in range(-1, GROUP + 1)]
        flux = [v[k] + h[k] * v[k] for k in range(GROUP + 2)]
        for k in range(1, GROUP + 1):
            f = f_ref[row + k - 1]
            t_h = dx(u[k] + h[k] * u[k]) + (flux[k + 1] - flux[k - 1])
            t_u = u[k] * dx(u[k]) + v[k] * ((u[k + 1] - u[k - 1]) - f) + dx(h[k])
            t_v = u[k] * (dx(v[k]) + f) + v[k] * (v[k + 1] - v[k - 1]) + (h[k + 1] - h[k - 1])
            for c, (now, t) in enumerate(((h[k], t_h), (u[k], t_u), (v[k], t_v))):
                new = now - (0.5 * time_step) * t
                if kind == 1:
                    new = 0.75 * load(base, c, k - 1) + 0.25 * new
                elif kind == 2:
                    new = (1.0 / 3.0) * load(base, c, k - 1) + (2.0 / 3.0) * new
                dst[c, pl.ds(pl.multiple_of((row + k - 1) * 8, 8), 8), :] = new
        return carry

    lax.fori_loop(0, -(-rows // GROUP), body, 0)


def run_model(bufs, f_ref, rows):
    x, b, c, y = bufs
    done = 0
    for _ in range(STEPS):
        for kind, (src, base, dst) in enumerate(((x, x, b), (b, x, c), (c, x, y))):
            done += 1
            stage(src, base, dst, f_ref, done, rows - 2 * done, kind)
        x, y = y, x
    return x


def pack_rows(out, src, out0, count, row0):
    for c in range(3):
        for r in range(0, count, 8):
            for s in range(8):
                out[c, out0 + r : out0 + r + 8, 128 * s : 128 * s + 128] = src[
                    c, pl.ds((row0 + r) * 8 + s, 8, stride=8), :
                ]


ROWS_1 = HALF + 2 * HALO
LOW_1 = MID - HALO


def first_model_kernel(f_ref, p0, p1, p2, p3, out, *bufs):
    for block, piece in enumerate((p0, p1, p2, p3)):
        for c in range(3):
            unpack_rows(bufs[0], piece.at[c], c, 0, FIRST, 0, block)
    views = [b.at[:, pl.ds(LOW_1 * 8, (ROWS_1 + 8) * 8), :] for b in bufs]
    done = run_model(views, f_ref, ROWS_1)
    pack_rows(out, done, 0, HALF, HALO)


TOP = MID + 2 * HALO
REST = ROWS - MID - HALF
BOTTOM = REST + 2 * HALO
ROWS_2 = TOP + BOTTOM


def second_model_kernel(f_ref, p0, p1, p2, p3, q0, q1, q2, q3, out, *bufs):
    x = bufs[0]
    late = ROWS - FIRST
    bottom = TOP + FIRST - (MID + HALF - HALO)
    for block, (p, q) in enumerate(((p0, q0), (p1, q1), (p2, q2), (p3, q3))):
        for c in range(3):
            edge = 3 * late + 2 * HALO * c
            unpack_rows(x, q, c, edge, 16, 0, block)
            unpack_rows(x, p.at[c], c, 0, 24, HALO, block)
            unpack_one_row(x, p.at[c], c, 24, HALO + 24, block)
            unpack_one_row(x, p.at[c], c, 71, TOP, block)
            unpack_rows(x, p.at[c], c, 72, 24, TOP + 1, block)
            unpack_rows(x, q, c, late * c, late, bottom, block)
            unpack_rows(x, q, c, edge + HALO, 8, bottom + late, block)
            unpack_one_row(x, q, c, edge + HALO + 8, bottom + late + 8, block)
    done = run_model(bufs, f_ref, ROWS_2)
    pack_rows(out, done, 0, MID, HALO)
    pack_rows(out, done, MID, REST, TOP + HALO)


def unpack_one_row(dst, piece, field, src_row, row, block):
    for half in range(2):
        dst[field, pl.ds(row * 8 + 2 * block + half, 1), :] = piece[
            src_row : src_row + 1, 128 * half : 128 * half + 128
        ]


def vmem_spec():
    return pl.BlockSpec(memory_space=pltpu.VMEM)


def smem_spec():
    return pl.BlockSpec(memory_space=pltpu.SMEM)


def model_call(kernel, f, pieces, buffer_rows, rows):
    n_ops = rows * 9 * 1024 * 60
    return pl.pallas_call(
        kernel,
        out_shape=jax.ShapeDtypeStruct((3, HALF, NLON), F32),
        in_specs=[smem_spec()] + [vmem_spec()] * len(pieces),
        out_specs=vmem_spec(),
        scratch_shapes=[pltpu.VMEM((3, buffer_rows * 8, 128), F32)] * 4,
        compiler_params=pltpu.CompilerParams(vmem_limit_bytes=32 << 20),
        cost_estimate=pl.CostEstimate(
            flops=n_ops, bytes_accessed=4 * 3 * NLON * rows * 2, transcendentals=0
        ),
    )(f, *pieces)


def cosine_table():
    m = np.arange(NLON // 2 + 1)
    n = np.arange(NLON)
    factor = np.where((m == 0) | (m == NLON // 2), 1.0, 2.0) / NLON
    angle = 2.0 * np.pi / NLON * ((m[:, None] * n[None, :]) % NLON)
    return (factor[:, None] * np.cos(angle)).astype(np.float32)


def split(x):
    high = x.astype(BF16)
    return high, (x - high.astype(F32)).astype(BF16)


def toeplitz(row, size, sign):
    full = pltpu.roll(jnp.broadcast_to(row, (size, size)), 0, 1, stride=1, stride_axis=0)
    if sign < 0:
        c = lax.broadcasted_iota(jnp.int32, (size, size), 0)
        r = lax.broadcasted_iota(jnp.int32, (size, size), 1)
        full = jnp.where(r < c, -full, full)
    return full


def matrices_kernel(a_ref, b_ref, r_ref, ah, al, bh, bl, rh, rl):
    for c in range(3):
        ah[c], al[c] = split(toeplitz(a_ref[c : c + 1, :], 256, 1))
        bh[c], bl[c] = split(toeplitz(b_ref[c : c + 1, :], 256, -1))
        rh[c], rl[c] = split(toeplitz(r_ref[c : c + 1, :], 512, -1))


def weighting_matrices(variances):
    k = jnp.dot(variances, jnp.asarray(cosine_table()), precision=lax.Precision.HIGHEST)
    k0, k1, k2, k3 = (k[:, 256 * j : 256 * j + 256] for j in range(4))
    even = (k0 + k2) * 0.25
    odd = (k1 + k3) * 0.25
    r = (k[:, :512] - k[:, 512:]) * 0.5
    shapes = [(3, n, n) for n in (256, 256, 256, 256, 512, 512)]
    return pl.pallas_call(
        matrices_kernel,
        out_shape=[jax.ShapeDtypeStruct(s, BF16) for s in shapes],
        in_specs=[vmem_spec()] * 3,
        out_specs=[vmem_spec()] * 6,
        compiler_params=pltpu.CompilerParams(vmem_limit_bytes=32 << 20),
    )(even + odd, even - odd, r)


def dot3(x, high, low):
    xh, xl = split(x)
    return (
        jnp.dot(xh, high, preferred_element_type=F32)
        + jnp.dot(xl, high, preferred_element_type=F32)
        + jnp.dot(xh, low, preferred_element_type=F32)
    )


def weight_kernel(pick, n_x, flag, f_ref, b_ref, *refs):
    x_refs = refs[:n_x]
    ah, al, bh, bl, rh, rl = refs[n_x : n_x + 6]
    outs = refs[n_x + 6 :]
    start = flag[0] != 0
    for c in range(3):
        d = []
        for block in range(4):
            cols = slice(256 * block, 256 * block + 256)
            f = f_ref[c, :, cols]
            back = b_ref[:, c, :, cols].reshape(HALF, 256)
            prev = jnp.where(start, back, f)
            d.append(pick(x_refs, block, c) - prev)
        even, odd = d[0] + d[2], d[1] + d[3]
        x = dot3(even + odd, ah[c], al[c])
        y = dot3(even - odd, bh[c], bl[c])
        w = dot3(
            jnp.concatenate([d[0] - d[2], d[1] - d[3]], axis=1), rh[c], rl[c]
        )
        w0, w1 = w[:, :256], w[:, 256:]
        p, q = x + y, x - y
        outs[0][c] = p + w0
        outs[1][c] = q + w1
        outs[2][c] = p - w0
        outs[3][c] = q - w1


def pick_first(refs, block, c):
    return refs[block][c, MID : MID + HALF, :]


def pick_second(refs, block, c):
    early, late = refs[block], refs[4 + block]
    return jnp.concatenate(
        [
            early[c, :MID, :],
            early[c, MID + HALF : FIRST, :],
            late[(ROWS - FIRST) * c : (ROWS - FIRST) * (c + 1), :],
        ],
        axis=0,
    )


def weight_call(pick, flag, f, back, xs, mats):
    return pl.pallas_call(
        functools.partial(weight_kernel, pick, len(xs)),
        out_shape=[jax.ShapeDtypeStruct((3, HALF, 256), F32)] * 4,
        in_specs=[smem_spec()] + [vmem_spec()] * (2 + len(xs) + 6),
        out_specs=[vmem_spec()] * 4,
        compiler_params=pltpu.CompilerParams(vmem_limit_bytes=32 << 20),
        cost_estimate=pl.CostEstimate(
            flops=2 * 3 * HALF * 6 * 256 * 256 * 3, bytes_accessed=8 << 20, transcendentals=0
        ),
    )(flag, f, back, *xs, *mats)


def coriolis_rows(total, first, offsets):
    index = (first + offsets).astype(F32)
    return 2.0 * coriolis_peak * jnp.sin(2.0 * jnp.pi * (index + 0.5) / total)


def ring(count, shift):
    return [(i, (i + shift) % count) for i in range(count)]


def to_next(value, j):
    pairs = [
        (s * LON + a, ((s + 1) % SUB) * LON + (a + j) % LON)
        for s in range(SUB)
        for a in range(LON)
    ]
    return lax.ppermute(value, ("sub", "lon"), pairs)


def to_lon(value, j):
    return lax.ppermute(value, "lon", ring(LON, j))


ORDER = (0, 3, 2, 1)


def shards(segment_launch_values, initial_backdrop, spectral_inverse_variances):
    x = segment_launch_values[0]
    sub, lat, lon = (lax.axis_index(n) for n in ("sub", "lat", "lon"))
    tile_rows = x.shape[1]
    total = tile_rows * lax.axis_size("lat")
    target = [lax.rem(lon + j, LON) for j in range(LON)]
    late = ROWS - FIRST

    above = lax.ppermute(x[:, tile_rows - HALO :], "lat", ring(8, 1))
    below = lax.ppermute(x[:, :HALO], "lat", ring(8, -1))

    p = {}
    for j in (2, 1, 3, 0):
        block = lax.dynamic_slice(x, (0, ROWS * target[j], 0), (3, FIRST, 256))
        p[j] = to_next(block, j)

    b = {}
    for j in (2, 1, 3, 0):
        part = lax.dynamic_slice(
            initial_backdrop, (0, ROWS * target[j] + 16 * sub, 0), (3, 16, 256)
        )
        b[j] = to_lon(part, j) if j else part
    back = lax.all_gather(jnp.concatenate([b[j] for j in ORDER], axis=2), "sub")

    edges = []
    for q in range(LON):
        up = above if q == 0 else x[:, ROWS * q - HALO : ROWS * q]
        down = below if q == LON - 1 else x[:, ROWS * (q + 1) : ROWS * (q + 1) + HALO]
        edges.append(jnp.concatenate([up, down], axis=1).reshape(6 * HALO, 256))
    edges = jnp.stack(edges)
    q = {}
    for j in (2, 1, 3, 0):
        rest = lax.dynamic_slice(x, (0, ROWS * target[j] + FIRST, 0), (3, late, 256))
        edge = lax.dynamic_index_in_dim(edges, target[j], 0, keepdims=False)
        q[j] = to_next(jnp.concatenate([rest.reshape(3 * late, 256), edge], axis=0), j)

    own_p = {j: lax.ppermute(p[j], "sub", ring(SUB, -1)) for j in (0, 1, 3, 2)}
    own_q = {j: lax.ppermute(q[j][: 3 * late], "sub", ring(SUB, -1)) for j in (0, 1, 3, 2)}

    mats = weighting_matrices(spectral_inverse_variances)
    flag = (sub == 0).astype(jnp.int32).reshape(1)
    first_row = lat * tile_rows + lon * ROWS

    ps = [p[j] for j in ORDER]
    qs = [q[j] for j in ORDER]
    own_ps = [own_p[j] for j in ORDER]
    own_qs = [own_q[j] for j in ORDER]

    f1 = coriolis_rows(total, first_row, LOW_1 + jnp.arange(ROWS_1 + 8))
    offsets = np.concatenate([np.arange(TOP) - HALO, np.arange(BOTTOM + 8) + MID + HALF - HALO])
    f2 = coriolis_rows(total, first_row, jnp.asarray(offsets))

    m1 = model_call(first_model_kernel, f1, ps, FIRST + 8, ROWS_1)
    o1 = weight_call(pick_first, flag, m1, back[1:5], own_ps, mats)
    r1 = [to_lon(o1[j], j) if j else o1[j] for j in range(LON)]
    m2 = model_call(second_model_kernel, f2, ps + qs, ROWS_2 + 16, ROWS_2)
    back2 = jnp.concatenate([back[:1], back[5:]], axis=0)
    o2 = weight_call(pick_second, flag, m2, back2, own_ps + own_qs, mats)
    r2 = [to_lon(o2[j], j) if j else o2[j] for j in range(LON)]

    out = jnp.zeros_like(x)
    for j in range(LON):
        row = ROWS * lax.rem(lon - j + LON, LON)
        out = lax.dynamic_update_slice(out, r1[j], (0, row + MID, 0))
        out = lax.dynamic_update_slice(out, r2[j][:, :MID], (0, row, 0))
        out = lax.dynamic_update_slice(out, r2[j][:, MID:], (0, row + MID + HALF, 0))
    return out[None]


def solution(mesh):
    return jax.shard_map(
        shards,
        mesh=mesh,
        in_specs=(P("sub", None, "lat", "lon"), P(None, "lat", "lon"), P()),
        out_specs=P("sub", None, "lat", "lon"),
        check_vma=False,
    )
```

```python
import functools

import numpy as np
import jax
import jax.numpy as jnp
from jax import lax
from jax.experimental import pallas as pl
from jax.experimental.pallas import tpu as pltpu
from jax.sharding import PartitionSpec as P

NLON = 1024
STEPS = 3
time_step = 0.5
coriolis_peak = 0.4

SUB = 8
LON = 4
ROWS = 128
HALO = 3 * STEPS
CHUNK = ROWS // 2
PART = ROWS // SUB
SENT = 440
TILES = CHUNK + 2 * HALO
GROUP = 16
SPARE = 2 * GROUP
F32 = jnp.float32
BF16 = jnp.bfloat16


def vmem_spec():
    return pl.BlockSpec(memory_space=pltpu.VMEM)


def smem_spec():
    return pl.BlockSpec(memory_space=pltpu.SMEM)


def hbm_spec():
    return pl.BlockSpec(memory_space=pltpu.HBM)


def call(kernel, outs, in_specs, out_specs, scratch, mib, **kwargs):
    return pl.pallas_call(
        kernel,
        out_shape=outs,
        in_specs=in_specs,
        out_specs=out_specs,
        scratch_shapes=scratch,
        compiler_params=pltpu.CompilerParams(vmem_limit_bytes=mib << 20),
        cost_estimate=pl.CostEstimate(flops=0, bytes_accessed=1, transcendentals=0),
        **kwargs,
    )


def array(*shape):
    return jax.ShapeDtypeStruct(shape, F32)


def dma_sems(n):
    return pltpu.SemaphoreType.DMA((n,))


def start_all(sem, pairs):
    copies = [pltpu.make_async_copy(a, b, sem.at[n]) for n, (a, b) in enumerate(pairs)]
    for copy in copies:
        copy.start()
    return copies


def aligned(row):
    return pl.multiple_of(row, 16)


def unpack_rows(dst, piece, field, first, count, row0, block):
    done = 0
    while done < count:
        n = min(8, count - done)
        for half in range(2):
            value = piece[first + done : first + done + n, 128 * half : 128 * half + 128]
            start = (row0 + done) * 8 + 2 * block + half
            where = pl.ds(start, n, stride=8) if n > 1 else pl.ds(start, 1)
            dst[field, where, :] = value + 1.0 if field == 0 else value
        done += n


def stage(src, base, dst, f_ref, lo, rows, kind):
    lane = lax.broadcasted_iota(jnp.int32, (8, 128), 1)
    is_first = lane == 0
    is_last = lane == 127

    def neighbours(a):
        up = pltpu.roll(a, 127, 1)
        down = pltpu.roll(a, 1, 1)
        up = jnp.where(is_last, pltpu.roll(up, 7, 0), up)
        down = jnp.where(is_first, pltpu.roll(down, 1, 0), down)
        return up, down

    def body(g, carry):
        row = lo + g * GROUP

        def load(ref, c, k):
            return ref[c, pl.ds(pl.multiple_of((row + k) * 8, 8), 8), :]

        d = [load(src, 0, k) for k in range(-1, GROUP + 1)]
        u = [load(src, 1, k) for k in range(-1, GROUP + 1)]
        v = [load(src, 2, k) for k in range(-1, GROUP + 1)]
        flux = [d[k] * v[k] for k in range(GROUP + 2)]
        for k in range(1, GROUP + 1):
            f = f_ref[row + k - 1]
            d_up, d_down = neighbours(d[k])
            u_up, u_down = neighbours(u[k])
            v_up, v_down = neighbours(v[k])
            t_h = (d_up * u_up - d_down * u_down) + (flux[k + 1] - flux[k - 1])
            t_u = u[k] * (u_up - u_down) + v[k] * ((u[k + 1] - u[k - 1]) - f) + (d_up - d_down)
            t_v = u[k] * ((v_up - v_down) + f) + v[k] * (v[k + 1] - v[k - 1]) + (d[k + 1] - d[k - 1])
            for c, (now, t) in enumerate(((d[k], t_h), (u[k], t_u), (v[k], t_v))):
                new = now - (0.5 * time_step) * t
                if kind == 1:
                    new = 0.75 * load(base, c, k - 1) + 0.25 * new
                elif kind == 2:
                    new = (1.0 / 3.0) * load(base, c, k - 1) + (2.0 / 3.0) * new
                dst[c, pl.ds(pl.multiple_of((row + k - 1) * 8, 8), 8), :] = new
        return carry

    lax.fori_loop(0, -(-rows // GROUP), body, 0)


def model_kernel(second, f_ref, s0, s3, s2, s1, out, *bufs):
    x, b, c, y = bufs
    for block, s in enumerate((s0, s3, s2, s1)):
        for field in range(3):
            row = ROWS * field
            edge = 3 * ROWS + 2 * HALO * field
            if second:
                unpack_rows(x, s, field, row + CHUNK - HALO, 1, 0, block)
                unpack_rows(x, s, field, row + CHUNK - HALO + 1, CHUNK + HALO - 1, 1, block)
                unpack_rows(x, s, field, edge + HALO, HALO, CHUNK + HALO, block)
            else:
                unpack_rows(x, s, field, edge, HALO, 0, block)
                unpack_rows(x, s, field, row, CHUNK + HALO, HALO, block)
    done = 0
    for _ in range(STEPS):
        for kind, (src, base, dst) in enumerate(((x, x, b), (b, x, c), (c, x, y))):
            done += 1
            stage(src, base, dst, f_ref, done, TILES - 2 * done, kind)
        x, y = y, x
    for field in range(3):
        for r in range(0, CHUNK, 8):
            for s in range(8):
                value = x[field, pl.ds((HALO + r) * 8 + s, 8, stride=8), :]
                out[field, r : r + 8, 128 * s : 128 * s + 128] = (
                    value - 1.0 if field == 0 else value
                )


def model_call(second, f, pieces):
    return call(
        functools.partial(model_kernel, second),
        array(3, CHUNK, NLON),
        [smem_spec()] + [vmem_spec()] * 4,
        vmem_spec(),
        [pltpu.VMEM((3, (TILES + SPARE) * 8, 128), F32)] * 4,
        10,
    )(f, *pieces)


def prepare_kernel(t_ref, x, back, b2, b1, b3, b0, last, first, sem):
    rows = x.shape[1]
    pairs = []
    for j, b in ((2, b2), (1, b1), (3, b3), (0, b0)):
        row = aligned(t_ref[j] * ROWS + t_ref[4] * PART)
        pairs.append((back.at[:, pl.ds(row, PART), :], b))
    pairs += [(x.at[:, pl.ds(rows - 16, 16), :], last), (x.at[:, pl.ds(0, 16), :], first)]
    for copy in start_all(sem, pairs):
        copy.wait()


def prepare(t, x, back):
    return call(
        prepare_kernel,
        [array(3, PART, 256)] * 4 + [array(3, 16, 256)] * 2,
        [smem_spec(), hbm_spec(), hbm_spec()],
        [vmem_spec()] * 6,
        [dma_sems(6)],
        60,
    )(t, x, back)


def send_kernel(t_ref, x, above, below, s2, s1, s3, s0, edges, sem):
    rows = x.shape[1]
    pairs = []
    for q in range(1, LON):
        pairs.append((x.at[:, pl.ds(ROWS * q - 16, 32), :], edges.at[q]))
    pairs += [
        (above, edges.at[0, :, pl.ds(0, 16), :]),
        (x.at[:, pl.ds(rows - 16, 16), :], edges.at[LON, :, pl.ds(0, 16), :]),
        (below, edges.at[LON, :, pl.ds(16, 16), :]),
    ]
    small = len(pairs)
    for j, s in ((2, s2), (1, s1), (3, s3), (0, s0)):
        for c in range(3):
            row = aligned(t_ref[j] * ROWS)
            pairs.append((x.at[c, pl.ds(row, ROWS), :], s.at[pl.ds(ROWS * c, ROWS), :]))
    copies = start_all(sem, pairs)
    for copy in copies[:small]:
        copy.wait()
    for j, s in ((2, s2), (1, s1), (3, s3), (0, s0)):
        for c in range(3):
            edge = 3 * ROWS + 2 * HALO * c
            s[edge : edge + HALO, :] = edges[t_ref[j], c, 16 - HALO : 16, :]
            s[edge + HALO : edge + 2 * HALO, :] = edges[t_ref[j] + 1, c, 16 : 16 + HALO, :]
    for copy in copies[small:]:
        copy.wait()


def send(t, x, above, below):
    return call(
        send_kernel,
        [array(SENT, 256)] * 4,
        [smem_spec()] + [hbm_spec()] * 3,
        [vmem_spec()] * 4,
        [pltpu.VMEM((LON + 1, 3, 32, 256), F32), dma_sems(18)],
        6,
    )(t, x, above, below)


def place_kernel(first, t_ref, o0, r1, r2, r3, *refs):
    out, sem = refs[-2:]
    pairs = [
        (r, out.at[:, pl.ds(aligned(t_ref[5 + j] * ROWS + first), CHUNK), :])
        for j, r in enumerate((o0, r1, r2, r3))
    ]
    for copy in start_all(sem, pairs):
        copy.wait()


def place(t, pieces, rows, begun=None):
    extra = [] if begun is None else [begun]
    return call(
        functools.partial(place_kernel, CHUNK if extra else 0),
        [array(3, rows, 256)],
        [smem_spec()] + [hbm_spec()] * (4 + len(extra)),
        [hbm_spec()],
        [dma_sems(4)],
        2,
        input_output_aliases={5: 0} if extra else {},
    )(t, *pieces, *extra)[0]


def cosine_table():
    m = np.arange(NLON // 2 + 1)
    n = np.arange(NLON)
    factor = np.where((m == 0) | (m == NLON // 2), 1.0, 2.0) / NLON
    angle = 2.0 * np.pi / NLON * ((m[:, None] * n[None, :]) % NLON)
    return (factor[:, None] * np.cos(angle)).astype(np.float32)


def split(x):
    high = x.astype(BF16)
    return high, (x - high.astype(F32)).astype(BF16)


def toeplitz(row, size, sign):
    full = pltpu.roll(jnp.broadcast_to(row, (size, size)), 0, 1, stride=1, stride_axis=0)
    if sign < 0:
        c = lax.broadcasted_iota(jnp.int32, (size, size), 0)
        r = lax.broadcasted_iota(jnp.int32, (size, size), 1)
        full = jnp.where(r < c, -full, full)
    return full


def weighting_rows(variances):
    k = jnp.dot(variances, jnp.asarray(cosine_table()), precision=lax.Precision.HIGHEST)
    k0, k1, k2, k3 = (k[:, 256 * j : 256 * j + 256] for j in range(4))
    even = (k0 + k2) * 0.25
    odd = (k1 + k3) * 0.25
    return even + odd, even - odd, (k[:, :512] - k[:, 512:]) * 0.5


def dot3(x, high, low):
    n = x.shape[0]
    xh, xl = split(x)
    y = jnp.dot(jnp.concatenate([xh, xl], axis=0), high, preferred_element_type=F32)
    return y[:n] + y[n:] + jnp.dot(xh, low, preferred_element_type=F32)


def weight_kernel(half, flag, f_ref, a_ref, b_ref, r_ref, back, w0, w3, w2, w1, *refs):
    outs = refs[:4]
    back_v, sem = refs[4:]
    parts = CHUNK // PART
    copies = start_all(sem, [(back.at[parts * half + n], back_v.at[n]) for n in range(parts)])
    start = flag[0] != 0
    for c in range(3):
        a = split(toeplitz(a_ref[c : c + 1, :], 256, 1))
        b = split(toeplitz(b_ref[c : c + 1, :], 256, -1))
        r = split(toeplitz(r_ref[c : c + 1, :], 512, -1))
        if c == 0:
            for copy in copies:
                copy.wait()
        d = []
        for block, own in enumerate((w0, w3, w2, w1)):
            rows = jnp.concatenate([back_v[n, block, c] for n in range(parts)], axis=0)
            prev = jnp.where(start, rows, f_ref[c, :, 256 * block : 256 * block + 256])
            row = ROWS * c + CHUNK * half
            d.append(own[row : row + CHUNK, :] - prev)
        even, odd = d[0] + d[2], d[1] + d[3]
        x = dot3(even + odd, *a)
        y = dot3(even - odd, *b)
        w = dot3(jnp.concatenate([d[0] - d[2], d[1] - d[3]], axis=1), *r)
        p, q = x + y, x - y
        outs[0][c] = p + w[:, :256]
        outs[1][c] = q + w[:, 256:]
        outs[2][c] = p - w[:, :256]
        outs[3][c] = q - w[:, 256:]


def weight_call(half, flag, f, back, own, rows):
    parts = CHUNK // PART
    return call(
        functools.partial(weight_kernel, half),
        [array(3, CHUNK, 256)] * 4,
        [smem_spec()] + [vmem_spec()] * 4 + [hbm_spec()] + [vmem_spec()] * 4,
        [vmem_spec()] * 4,
        [pltpu.VMEM((parts, 4, 3, PART, 256), F32), dma_sems(parts)],
        10,
    )(flag, f, *rows, back, *own)


def coriolis_rows(total, first, offsets):
    index = (first + offsets).astype(F32)
    return 2.0 * coriolis_peak * jnp.sin(2.0 * jnp.pi * (index + 0.5) / total)


def ring(count, shift):
    return [(i, (i + shift) % count) for i in range(count)]


def to_next(value, j):
    pairs = [
        (s * LON + a, ((s + 1) % SUB) * LON + (a + j) % LON)
        for s in range(SUB)
        for a in range(LON)
    ]
    return lax.ppermute(value, ("sub", "lon"), pairs)


def to_lon(value, j):
    return lax.ppermute(value, "lon", ring(LON, j))


ORDER = (0, 3, 2, 1)


def shards(segment_launch_values, initial_backdrop, spectral_inverse_variances):
    x = segment_launch_values[0]
    sub, lat, lon = (lax.axis_index(n) for n in ("sub", "lat", "lon"))
    tile_rows = x.shape[1]
    total = tile_rows * lax.axis_size("lat")
    t = jnp.stack(
        [lax.rem(lon + j, LON) for j in range(LON)]
        + [sub]
        + [lax.rem(lon - j + LON, LON) for j in range(LON)]
    )

    *parts, last, first = prepare(t, x, initial_backdrop)
    above = lax.ppermute(last, "lat", ring(8, 1))
    below = lax.ppermute(first, "lat", ring(8, -1))
    b2, b1, b3 = (to_lon(v, j) for v, j in zip(parts, (2, 1, 3)))
    back = lax.all_gather(jnp.stack([parts[3], b3, b2, b1]), "sub")

    flag = (sub == 0).astype(jnp.int32).reshape(1)
    first_row = lat * tile_rows + lon * ROWS
    offsets = jnp.arange(TILES + SPARE) - HALO
    f1 = coriolis_rows(total, first_row, offsets)
    f2 = coriolis_rows(total, first_row, offsets + CHUNK)
    rows = weighting_rows(spectral_inverse_variances)
    above, *tied = lax.optimization_barrier((above, f1, f2, flag, *rows))
    f1, f2, flag, *rows = tied

    sent = send(t, x, above, below)
    s2, s1, s3, s0 = (to_next(v, j) for v, j in zip(sent, (2, 1, 3, 0)))
    come = [s0, s3, s2, s1]
    own = [lax.ppermute(v, "sub", ring(SUB, -1)) for v in come]

    m1 = model_call(False, f1, come)
    o1 = weight_call(0, flag, m1, back, own, rows)
    r1 = [to_lon(o1[j], j) if j else o1[j] for j in range(LON)]
    f2, *o1 = lax.optimization_barrier((f2, *o1))
    m2 = model_call(True, f2, come)
    o2 = weight_call(1, flag, m2, back, own, rows)
    r2 = [to_lon(o2[j], j) if j else o2[j] for j in range(LON)]
    return place(t, r2, tile_rows, place(t, r1, tile_rows))[None]


def solution(mesh):
    return jax.shard_map(
        shards,
        mesh=mesh,
        in_specs=(P("sub", None, "lat", "lon"), P(None, "lat", "lon"), P()),
        out_specs=P("sub", None, "lat", "lon"),
        check_vma=False,
    )
```

```python
import functools

import numpy as np
import jax
import jax.numpy as jnp
from jax import lax
from jax.experimental import pallas as pl
from jax.experimental.pallas import tpu as pltpu
from jax.sharding import PartitionSpec as P

NLON = 1024
STEPS = 3
time_step = 0.5
coriolis_peak = 0.4

SUB = 8
LON = 4
ROWS = 128
HALO = 3 * STEPS
CHUNK = ROWS // 2
SENT = 440
TILES = CHUNK + 2 * HALO
GROUP = 16
SPARE = 2 * GROUP
F32 = jnp.float32
BF16 = jnp.bfloat16


def vmem_spec():
    return pl.BlockSpec(memory_space=pltpu.VMEM)


def smem_spec():
    return pl.BlockSpec(memory_space=pltpu.SMEM)


def hbm_spec():
    return pl.BlockSpec(memory_space=pltpu.HBM)


def call(kernel, outs, in_specs, out_specs, scratch, mib, **kwargs):
    return pl.pallas_call(
        kernel,
        out_shape=outs,
        in_specs=in_specs,
        out_specs=out_specs,
        scratch_shapes=scratch,
        compiler_params=pltpu.CompilerParams(vmem_limit_bytes=mib << 20),
        cost_estimate=pl.CostEstimate(flops=0, bytes_accessed=1, transcendentals=0),
        **kwargs,
    )


def array(*shape):
    return jax.ShapeDtypeStruct(shape, F32)


def dma_sems(n):
    return pltpu.SemaphoreType.DMA((n,))


def start_all(sem, pairs):
    copies = [pltpu.make_async_copy(a, b, sem.at[n]) for n, (a, b) in enumerate(pairs)]
    for copy in copies:
        copy.start()
    return copies


def aligned(row):
    return pl.multiple_of(row, 16)


def unpack_rows(dst, piece, field, first, count, row0, block):
    done = 0
    while done < count:
        n = min(8, count - done)
        for half in range(2):
            value = piece[first + done : first + done + n, 128 * half : 128 * half + 128]
            start = (row0 + done) * 8 + 2 * block + half
            where = pl.ds(start, n, stride=8) if n > 1 else pl.ds(start, 1)
            dst[field, where, :] = value + 1.0 if field == 0 else value
        done += n


def stage(src, base, dst, f_ref, lo, rows, kind):
    lane = lax.broadcasted_iota(jnp.int32, (8, 128), 1)
    is_first = lane == 0
    is_last = lane == 127

    def neighbours(a):
        up = pltpu.roll(a, 127, 1)
        down = pltpu.roll(a, 1, 1)
        up = jnp.where(is_last, pltpu.roll(up, 7, 0), up)
        down = jnp.where(is_first, pltpu.roll(down, 1, 0), down)
        return up, down

    def body(g, carry):
        row = lo + g * GROUP

        def load(ref, c, k):
            return ref[c, pl.ds(pl.multiple_of((row + k) * 8, 8), 8), :]

        d = [load(src, 0, k) for k in range(-1, GROUP + 1)]
        u = [load(src, 1, k) for k in range(-1, GROUP + 1)]
        v = [load(src, 2, k) for k in range(-1, GROUP + 1)]
        flux = [d[k] * v[k] for k in range(GROUP + 2)]
        for k in range(1, GROUP + 1):
            f = f_ref[row + k - 1]
            d_up, d_down = neighbours(d[k])
            u_up, u_down = neighbours(u[k])
            v_up, v_down = neighbours(v[k])
            t_h = (d_up * u_up - d_down * u_down) + (flux[k + 1] - flux[k - 1])
            t_u = u[k] * (u_up - u_down) + v[k] * ((u[k + 1] - u[k - 1]) - f) + (d_up - d_down)
            t_v = u[k] * ((v_up - v_down) + f) + v[k] * (v[k + 1] - v[k - 1]) + (d[k + 1] - d[k - 1])
            for c, (now, t) in enumerate(((d[k], t_h), (u[k], t_u), (v[k], t_v))):
                new = now - (0.5 * time_step) * t
                if kind == 1:
                    new = 0.75 * load(base, c, k - 1) + 0.25 * new
                elif kind == 2:
                    new = (1.0 / 3.0) * load(base, c, k - 1) + (2.0 / 3.0) * new
                dst[c, pl.ds(pl.multiple_of((row + k - 1) * 8, 8), 8), :] = new
        return carry

    lax.fori_loop(0, -(-rows // GROUP), body, 0)


def model_kernel(second, f_ref, s0, s3, s2, s1, out, *bufs):
    x, b, c, y = bufs
    for block, s in enumerate((s0, s3, s2, s1)):
        for field in range(3):
            row = ROWS * field
            edge = 3 * ROWS + 2 * HALO * field
            if second:
                unpack_rows(x, s, field, row + CHUNK - HALO, 1, 0, block)
                unpack_rows(x, s, field, row + CHUNK - HALO + 1, CHUNK + HALO - 1, 1, block)
                unpack_rows(x, s, field, edge + HALO, HALO, CHUNK + HALO, block)
            else:
                unpack_rows(x, s, field, edge, HALO, 0, block)
                unpack_rows(x, s, field, row, CHUNK + HALO, HALO, block)
    done = 0
    for _ in range(STEPS):
        for kind, (src, base, dst) in enumerate(((x, x, b), (b, x, c), (c, x, y))):
            done += 1
            stage(src, base, dst, f_ref, done, TILES - 2 * done, kind)
        x, y = y, x
    for field in range(3):
        for r in range(0, CHUNK, 8):
            for s in range(8):
                value = x[field, pl.ds((HALO + r) * 8 + s, 8, stride=8), :]
                out[field, r : r + 8, 128 * s : 128 * s + 128] = (
                    value - 1.0 if field == 0 else value
                )


def model_call(second, f, pieces):
    return call(
        functools.partial(model_kernel, second),
        array(3, CHUNK, NLON),
        [smem_spec()] + [vmem_spec()] * 4,
        vmem_spec(),
        [pltpu.VMEM((3, (TILES + SPARE) * 8, 128), F32)] * 4,
        10,
    )(f, *pieces)


def rows_kernel(t_ref, x, s2, s1, s3, s0, sem):
    pairs = []
    for j, s in ((2, s2), (1, s1), (3, s3), (0, s0)):
        for c in range(3):
            row = aligned(t_ref[j] * ROWS)
            pairs.append((x.at[c, pl.ds(row, ROWS), :], s.at[pl.ds(ROWS * c, ROWS), :]))
    for copy in start_all(sem, pairs):
        copy.wait()
    for s in (s2, s1, s3, s0):
        s[3 * ROWS :, :] = jnp.zeros((SENT - 3 * ROWS, 256), F32)


def rows_to_send(t, x):
    return call(
        rows_kernel,
        [array(SENT, 256)] * 4,
        [smem_spec(), hbm_spec()],
        [vmem_spec()] * 4,
        [dma_sems(12)],
        60,
    )(t, x)


def edges_kernel(t_ref, x, above, below, *refs):
    outs = refs[4:8]
    edges, ready, sem, sem_out = refs[8:]
    rows = x.shape[1]
    pairs = []
    for q in range(1, LON):
        pairs.append((x.at[:, pl.ds(ROWS * q - 16, 32), :], edges.at[q]))
    pairs += [
        (x.at[:, pl.ds(0, 16), :], edges.at[0, :, pl.ds(16, 16), :]),
        (above, edges.at[0, :, pl.ds(0, 16), :]),
        (x.at[:, pl.ds(rows - 16, 16), :], edges.at[LON, :, pl.ds(0, 16), :]),
        (below, edges.at[LON, :, pl.ds(16, 16), :]),
    ]
    for copy in start_all(sem, pairs):
        copy.wait()
    pairs = []
    for n, j in enumerate((2, 1, 3, 0)):
        for c in range(3):
            edge = 2 * HALO * c
            ready[n, edge : edge + HALO, :] = edges[t_ref[j], c, 16 - HALO : 16, :]
            ready[n, edge + HALO : edge + 2 * HALO, :] = edges[t_ref[j] + 1, c, 16 : 16 + HALO, :]
        ready[n, 6 * HALO :, :] = jnp.zeros((SENT - 3 * ROWS - 6 * HALO, 256), F32)
        pairs.append((ready.at[n], outs[n].at[pl.ds(3 * ROWS, SENT - 3 * ROWS), :]))
    for copy in start_all(sem_out, pairs):
        copy.wait()


def add_edges(t, x, above, below, sent):
    return call(
        edges_kernel,
        [array(SENT, 256)] * 4,
        [smem_spec()] + [hbm_spec()] * 7,
        [hbm_spec()] * 4,
        [
            pltpu.VMEM((LON + 1, 3, 32, 256), F32),
            pltpu.VMEM((4, SENT - 3 * ROWS, 256), F32),
            dma_sems(7),
            dma_sems(4),
        ],
        60,
        input_output_aliases={4: 0, 5: 1, 6: 2, 7: 3},
    )(t, x, above, below, *sent)


def place_kernel(first, t_ref, o0, r1, r2, r3, *refs):
    out, sem = refs[-2:]
    pairs = [
        (r, out.at[:, pl.ds(aligned(t_ref[LON + j] * ROWS + first), CHUNK), :])
        for j, r in enumerate((o0, r1, r2, r3))
    ]
    for copy in start_all(sem, pairs):
        copy.wait()


def place(t, pieces, rows, begun=None):
    extra = [] if begun is None else [begun]
    return call(
        functools.partial(place_kernel, CHUNK if extra else 0),
        [array(3, rows, 256)],
        [smem_spec()] + [hbm_spec()] * (4 + len(extra)),
        [hbm_spec()],
        [dma_sems(4)],
        2,
        input_output_aliases={5: 0} if extra else {},
    )(t, *pieces, *extra)[0]


def cosine_table():
    m = np.arange(NLON // 2 + 1)
    n = np.arange(NLON)
    factor = np.where((m == 0) | (m == NLON // 2), 1.0, 2.0) / NLON
    angle = 2.0 * np.pi / NLON * ((m[:, None] * n[None, :]) % NLON)
    return (factor[:, None] * np.cos(angle)).astype(np.float32)


def split(x):
    high = x.astype(BF16)
    return high, (x - high.astype(F32)).astype(BF16)


def toeplitz(row, size, sign):
    full = pltpu.roll(jnp.broadcast_to(row, (size, size)), 0, 1, stride=1, stride_axis=0)
    if sign < 0:
        c = lax.broadcasted_iota(jnp.int32, (size, size), 0)
        r = lax.broadcasted_iota(jnp.int32, (size, size), 1)
        full = jnp.where(r < c, -full, full)
    return full


def weighting_rows(variances):
    k = jnp.dot(variances, jnp.asarray(cosine_table()), precision=lax.Precision.HIGHEST)
    k0, k1, k2, k3 = (k[:, 256 * j : 256 * j + 256] for j in range(4))
    even = (k0 + k2) * 0.25
    odd = (k1 + k3) * 0.25
    return even + odd, even - odd, (k[:, :512] - k[:, 512:]) * 0.5


def dot3(x, high, low):
    n = x.shape[0]
    xh, xl = split(x)
    y = jnp.dot(jnp.concatenate([xh, xl], axis=0), high, preferred_element_type=F32)
    return y[:n] + y[n:] + jnp.dot(xh, low, preferred_element_type=F32)


def weight_kernel(half, flag, f_ref, a_ref, b_ref, r_ref, *refs):
    own, back, outs = refs[:4], refs[4:8], refs[8:]
    start = flag[0] != 0
    rows = slice(CHUNK * half, CHUNK * half + CHUNK)
    for c in range(3):
        a = split(toeplitz(a_ref[c : c + 1, :], 256, 1))
        b = split(toeplitz(b_ref[c : c + 1, :], 256, -1))
        r = split(toeplitz(r_ref[c : c + 1, :], 512, -1))
        d = []
        for block in range(4):
            f = f_ref[c, :, 256 * block : 256 * block + 256]
            row = ROWS * c + CHUNK * half
            prev = jnp.where(start, back[block][c, rows, :], f)
            d.append(own[block][row : row + CHUNK, :] - prev)
        even, odd = d[0] + d[2], d[1] + d[3]
        x = dot3(even + odd, *a)
        y = dot3(even - odd, *b)
        w = dot3(jnp.concatenate([d[0] - d[2], d[1] - d[3]], axis=1), *r)
        p, q = x + y, x - y
        outs[0][c] = p + w[:, :256]
        outs[1][c] = q + w[:, 256:]
        outs[2][c] = p - w[:, :256]
        outs[3][c] = q - w[:, 256:]


def weight_call(half, flag, f, back, own, rows):
    return call(
        functools.partial(weight_kernel, half),
        [array(3, CHUNK, 256)] * 4,
        [smem_spec()] + [vmem_spec()] * 12,
        [vmem_spec()] * 4,
        [],
        10,
    )(flag, f, *rows, *own, *back)


def coriolis_rows(total, first, offsets):
    index = (first + offsets).astype(F32)
    return 2.0 * coriolis_peak * jnp.sin(2.0 * jnp.pi * (index + 0.5) / total)


def ring(count, shift):
    return [(i, (i + shift) % count) for i in range(count)]


def to_next(value, j):
    pairs = [
        (s * LON + a, ((s + 1) % SUB) * LON + (a + j) % LON)
        for s in range(SUB)
        for a in range(LON)
    ]
    return lax.ppermute(value, ("sub", "lon"), pairs)


def to_lon(value, j):
    return lax.ppermute(value, "lon", ring(LON, j))


ORDER = (0, 3, 2, 1)


def shards(segment_launch_values, initial_backdrop, spectral_inverse_variances):
    x = segment_launch_values[0]
    sub, lat, lon = (lax.axis_index(n) for n in ("sub", "lat", "lon"))
    tile_rows = x.shape[1]
    total = tile_rows * lax.axis_size("lat")
    t = jnp.stack(
        [lax.rem(lon + j, LON) for j in range(LON)]
        + [lax.rem(lon - j + LON, LON) for j in range(LON)]
    )

    above = lax.ppermute(x[:, tile_rows - 16 :], "lat", ring(8, 1))
    below = lax.ppermute(x[:, :16], "lat", ring(8, -1))

    flag = (sub == 0).astype(jnp.int32).reshape(1)
    first_row = lat * tile_rows + lon * ROWS
    offsets = jnp.arange(TILES + SPARE) - HALO
    f1 = coriolis_rows(total, first_row, offsets)
    f2 = coriolis_rows(total, first_row, offsets + CHUNK)
    rows = weighting_rows(spectral_inverse_variances)
    above, *tied = lax.optimization_barrier((above, f1, f2, flag, *rows))
    f1, f2, flag, *rows = tied

    sent = add_edges(t, x, above, below, rows_to_send(t, x))
    s2, s1, s3, s0 = (to_next(v, j) for v, j in zip(sent, (2, 1, 3, 0)))
    come = [s0, s3, s2, s1]
    own = [lax.ppermute(v, "sub", ring(SUB, -1)) for v in come]
    back = {}
    for j in (2, 1, 3, 0):
        block = lax.dynamic_slice(initial_backdrop, (0, ROWS * t[j], 0), (3, ROWS, 256))
        back[j] = lax.ppermute(block, ("sub", "lon"), ring(LON, j)) if j else block
    back = [back[j] for j in (0, 3, 2, 1)]

    m1 = model_call(False, f1, come)
    o1 = weight_call(0, flag, m1, back, own, rows)
    r1 = [to_lon(o1[j], j) if j else o1[j] for j in range(LON)]
    f2, *o1 = lax.optimization_barrier((f2, *o1))
    m2 = model_call(True, f2, come)
    o2 = weight_call(1, flag, m2, back, own, rows)
    r2 = [to_lon(o2[j], j) if j else o2[j] for j in range(LON)]
    return place(t, r2, tile_rows, place(t, r1, tile_rows))[None]


def solution(mesh):
    return jax.shard_map(
        shards,
        mesh=mesh,
        in_specs=(P("sub", None, "lat", "lon"), P(None, "lat", "lon"), P()),
        out_specs=P("sub", None, "lat", "lon"),
        check_vma=False,
    )
```

```python
import functools

import numpy as np
import jax
import jax.numpy as jnp
from jax import lax
from jax.experimental import pallas as pl
from jax.experimental.pallas import tpu as pltpu
from jax.sharding import PartitionSpec as P

NLON = 1024
STEPS = 3
time_step = 0.5
coriolis_peak = 0.4

SUB = 8
LON = 4
ROWS = 128
HALO = 3 * STEPS
CHUNK = ROWS // 2
SENT = 440
TILES = CHUNK + 2 * HALO
GROUP = 16
SPARE = 2 * GROUP
F32 = jnp.float32
BF16 = jnp.bfloat16


def vmem_spec():
    return pl.BlockSpec(memory_space=pltpu.VMEM)


def smem_spec():
    return pl.BlockSpec(memory_space=pltpu.SMEM)


def hbm_spec():
    return pl.BlockSpec(memory_space=pltpu.HBM)


def call(kernel, outs, in_specs, out_specs, scratch, mib, **kwargs):
    return pl.pallas_call(
        kernel,
        out_shape=outs,
        in_specs=in_specs,
        out_specs=out_specs,
        scratch_shapes=scratch,
        compiler_params=pltpu.CompilerParams(vmem_limit_bytes=mib << 20),
        cost_estimate=pl.CostEstimate(flops=0, bytes_accessed=1, transcendentals=0),
        **kwargs,
    )


def array(*shape):
    return jax.ShapeDtypeStruct(shape, F32)


def dma_sems(n):
    return pltpu.SemaphoreType.DMA((n,))


def start_all(sem, pairs):
    copies = [pltpu.make_async_copy(a, b, sem.at[n]) for n, (a, b) in enumerate(pairs)]
    for copy in copies:
        copy.start()
    return copies


def aligned(row):
    return pl.multiple_of(row, 16)


def unpack_rows(dst, piece, field, first, count, row0, block):
    done = 0
    while done < count:
        n = min(8, count - done)
        for half in range(2):
            value = piece[first + done : first + done + n, 128 * half : 128 * half + 128]
            start = (row0 + done) * 8 + 2 * block + half
            where = pl.ds(start, n, stride=8) if n > 1 else pl.ds(start, 1)
            dst[field, where, :] = value + 1.0 if field == 0 else value
        done += n


def stage(src, base, dst, f_ref, lo, rows, kind):
    lane = lax.broadcasted_iota(jnp.int32, (8, 128), 1)
    is_first = lane == 0
    is_last = lane == 127

    def neighbours(a):
        up = pltpu.roll(a, 127, 1)
        down = pltpu.roll(a, 1, 1)
        up = jnp.where(is_last, pltpu.roll(up, 7, 0), up)
        down = jnp.where(is_first, pltpu.roll(down, 1, 0), down)
        return up, down

    def body(g, carry):
        row = lo + g * GROUP

        def load(ref, c, k):
            return ref[c, pl.ds(pl.multiple_of((row + k) * 8, 8), 8), :]

        d = [load(src, 0, k) for k in range(-1, GROUP + 1)]
        u = [load(src, 1, k) for k in range(-1, GROUP + 1)]
        v = [load(src, 2, k) for k in range(-1, GROUP + 1)]
        flux = [d[k] * v[k] for k in range(GROUP + 2)]
        for k in range(1, GROUP + 1):
            f = f_ref[row + k - 1]
            d_up, d_down = neighbours(d[k])
            u_up, u_down = neighbours(u[k])
            v_up, v_down = neighbours(v[k])
            t_h = (d_up * u_up - d_down * u_down) + (flux[k + 1] - flux[k - 1])
            t_u = u[k] * (u_up - u_down) + v[k] * ((u[k + 1] - u[k - 1]) - f) + (d_up - d_down)
            t_v = u[k] * ((v_up - v_down) + f) + v[k] * (v[k + 1] - v[k - 1]) + (d[k + 1] - d[k - 1])
            for c, (now, t) in enumerate(((d[k], t_h), (u[k], t_u), (v[k], t_v))):
                new = now - (0.5 * time_step) * t
                if kind == 1:
                    new = 0.75 * load(base, c, k - 1) + 0.25 * new
                elif kind == 2:
                    new = (1.0 / 3.0) * load(base, c, k - 1) + (2.0 / 3.0) * new
                dst[c, pl.ds(pl.multiple_of((row + k - 1) * 8, 8), 8), :] = new
        return carry

    lax.fori_loop(0, -(-rows // GROUP), body, 0)


def model_kernel(second, f_ref, s0, s3, s2, s1, out, *bufs):
    x, b, c, y = bufs
    for block, s in enumerate((s0, s3, s2, s1)):
        for field in range(3):
            row = ROWS * field
            edge = 3 * ROWS + 2 * HALO * field
            if second:
                unpack_rows(x, s, field, row + CHUNK - HALO, 1, 0, block)
                unpack_rows(x, s, field, row + CHUNK - HALO + 1, CHUNK + HALO - 1, 1, block)
                unpack_rows(x, s, field, edge + HALO, HALO, CHUNK + HALO, block)
            else:
                unpack_rows(x, s, field, edge, HALO, 0, block)
                unpack_rows(x, s, field, row, CHUNK + HALO, HALO, block)
    done = 0
    for _ in range(STEPS):
        for kind, (src, base, dst) in enumerate(((x, x, b), (b, x, c), (c, x, y))):
            done += 1
            stage(src, base, dst, f_ref, done, TILES - 2 * done, kind)
        x, y = y, x
    for field in range(3):
        for r in range(0, CHUNK, 8):
            for s in range(8):
                value = x[field, pl.ds((HALO + r) * 8 + s, 8, stride=8), :]
                out[field, r : r + 8, 128 * s : 128 * s + 128] = (
                    value - 1.0 if field == 0 else value
                )


def model_call(second, f, pieces):
    return call(
        functools.partial(model_kernel, second),
        array(3, CHUNK, NLON),
        [smem_spec()] + [vmem_spec()] * 4,
        vmem_spec(),
        [pltpu.VMEM((3, (TILES + SPARE) * 8, 128), F32)] * 4,
        10,
    )(f, *pieces)


def rows_kernel(t_ref, x, back, s2, s1, s3, s0, e2, e1, e3, e0, sem, sem_extra):
    order = ((2, s2, e2), (1, s1, e1), (3, s3, e3), (0, s0, e0))
    at = [aligned(t_ref[j] * ROWS) for j, _, _ in order]
    pairs = []
    for row, (_, s, _) in zip(at, order):
        for c in range(3):
            pairs.append((x.at[c, pl.ds(row, ROWS), :], s.at[pl.ds(ROWS * c, ROWS), :]))
    copies = start_all(sem, pairs)

    @pl.when(t_ref[2 * LON] == 0)
    def _():
        pairs = [
            (back.at[:, pl.ds(aligned(row + CHUNK), CHUNK), :], e)
            for row, (_, _, e) in zip(at, order)
        ]
        for copy in start_all(sem_extra, pairs):
            copy.wait()

    @pl.when(t_ref[2 * LON] == SUB - 1)
    def _():
        pairs = [(x.at[:, pl.ds(row, CHUNK), :], e) for row, (_, _, e) in zip(at, order)]
        for copy in start_all(sem_extra, pairs):
            copy.wait()

    for copy in copies:
        copy.wait()

    @pl.when(t_ref[2 * LON] == SUB - 1)
    def _():
        pairs = []
        for row, (_, s, _) in zip(at, order):
            for c in range(3):
                pairs.append((back.at[c, pl.ds(row, CHUNK), :], s.at[pl.ds(ROWS * c, CHUNK), :]))
        for copy in start_all(sem, pairs):
            copy.wait()

    for _, s, _ in order:
        s[3 * ROWS :, :] = jnp.zeros((SENT - 3 * ROWS, 256), F32)


def rows_to_send(t, x, back):
    out = call(
        rows_kernel,
        [array(SENT, 256)] * 4 + [array(3, CHUNK, 256)] * 4,
        [smem_spec(), hbm_spec(), hbm_spec()],
        [vmem_spec()] * 8,
        [dma_sems(12), dma_sems(4)],
        60,
    )(t, x, back)
    return out[:4], out[4:]


def edges_kernel(t_ref, x, above, below, *refs):
    outs = refs[4:8]
    edges, ready, sem, sem_out = refs[8:]
    rows = x.shape[1]
    pairs = []
    for q in range(1, LON):
        pairs.append((x.at[:, pl.ds(ROWS * q - 16, 32), :], edges.at[q]))
    pairs += [
        (x.at[:, pl.ds(0, 16), :], edges.at[0, :, pl.ds(16, 16), :]),
        (above, edges.at[0, :, pl.ds(0, 16), :]),
        (x.at[:, pl.ds(rows - 16, 16), :], edges.at[LON, :, pl.ds(0, 16), :]),
        (below, edges.at[LON, :, pl.ds(16, 16), :]),
    ]
    for copy in start_all(sem, pairs):
        copy.wait()
    pairs = []
    for n, j in enumerate((2, 1, 3, 0)):
        for c in range(3):
            edge = 2 * HALO * c
            ready[n, edge : edge + HALO, :] = edges[t_ref[j], c, 16 - HALO : 16, :]
            ready[n, edge + HALO : edge + 2 * HALO, :] = edges[t_ref[j] + 1, c, 16 : 16 + HALO, :]
        ready[n, 6 * HALO :, :] = jnp.zeros((SENT - 3 * ROWS - 6 * HALO, 256), F32)
        pairs.append((ready.at[n], outs[n].at[pl.ds(3 * ROWS, SENT - 3 * ROWS), :]))
    for copy in start_all(sem_out, pairs):
        copy.wait()


def add_edges(t, x, above, below, sent):
    return call(
        edges_kernel,
        [array(SENT, 256)] * 4,
        [smem_spec()] + [hbm_spec()] * 7,
        [hbm_spec()] * 4,
        [
            pltpu.VMEM((LON + 1, 3, 32, 256), F32),
            pltpu.VMEM((4, SENT - 3 * ROWS, 256), F32),
            dma_sems(7),
            dma_sems(4),
        ],
        60,
        input_output_aliases={4: 0, 5: 1, 6: 2, 7: 3},
    )(t, x, above, below, *sent)


def place_kernel(first, t_ref, o0, r1, r2, r3, *refs):
    out, sem = refs[-2:]
    pairs = [
        (r, out.at[:, pl.ds(aligned(t_ref[LON + j] * ROWS + first), CHUNK), :])
        for j, r in enumerate((o0, r1, r2, r3))
    ]
    for copy in start_all(sem, pairs):
        copy.wait()


def place(t, pieces, rows, begun=None):
    extra = [] if begun is None else [begun]
    return call(
        functools.partial(place_kernel, CHUNK if extra else 0),
        [array(3, rows, 256)],
        [smem_spec()] + [hbm_spec()] * (4 + len(extra)),
        [hbm_spec()],
        [dma_sems(4)],
        2,
        input_output_aliases={5: 0} if extra else {},
    )(t, *pieces, *extra)[0]


def cosine_table():
    m = np.arange(NLON // 2 + 1)
    n = np.arange(NLON)
    factor = np.where((m == 0) | (m == NLON // 2), 1.0, 2.0) / NLON
    angle = 2.0 * np.pi / NLON * ((m[:, None] * n[None, :]) % NLON)
    return (factor[:, None] * np.cos(angle)).astype(np.float32)


def split(x):
    high = x.astype(BF16)
    return high, (x - high.astype(F32)).astype(BF16)


def toeplitz(row, size, sign):
    full = pltpu.roll(jnp.broadcast_to(row, (size, size)), 0, 1, stride=1, stride_axis=0)
    if sign < 0:
        c = lax.broadcasted_iota(jnp.int32, (size, size), 0)
        r = lax.broadcasted_iota(jnp.int32, (size, size), 1)
        full = jnp.where(r < c, -full, full)
    return full


def weighting_rows(variances):
    k = jnp.dot(variances, jnp.asarray(cosine_table()), precision=lax.Precision.HIGHEST)
    k0, k1, k2, k3 = (k[:, 256 * j : 256 * j + 256] for j in range(4))
    even = (k0 + k2) * 0.25
    odd = (k1 + k3) * 0.25
    return even + odd, even - odd, (k[:, :512] - k[:, 512:]) * 0.5


def dot3(x, high, low):
    n = x.shape[0]
    xh, xl = split(x)
    y = jnp.dot(jnp.concatenate([xh, xl], axis=0), high, preferred_element_type=F32)
    return y[:n] + y[n:] + jnp.dot(xh, low, preferred_element_type=F32)


def weight_kernel(half, t_ref, f_ref, a_ref, b_ref, r_ref, x, *refs):
    own, extra = refs[:3], refs[3:7]
    come = refs[7:11] if half == 0 else None
    outs = refs[-6:-2]
    mine, sem = refs[-2:]
    copy = pltpu.make_async_copy(
        x.at[:, pl.ds(aligned(t_ref[0] * ROWS + CHUNK * half), CHUNK), :], mine, sem.at[0]
    )
    copy.start()
    first = t_ref[2 * LON] == 0
    last = t_ref[2 * LON] == SUB - 1
    for c in range(3):
        a = split(toeplitz(a_ref[c : c + 1, :], 256, 1))
        b = split(toeplitz(b_ref[c : c + 1, :], 256, -1))
        r = split(toeplitz(r_ref[c : c + 1, :], 512, -1))
        if c == 0:
            copy.wait()
        d = []
        row = ROWS * c + CHUNK * half
        for block in range(4):
            f = f_ref[c, :, 256 * block : 256 * block + 256]
            now = mine[c] if block == 0 else own[block - 1][row : row + CHUNK, :]
            if half == 0:
                if block:
                    now = jnp.where(last, extra[block][c], now)
                prev = jnp.where(first, come[block][row : row + CHUNK, :], f)
            else:
                prev = jnp.where(first, extra[block][c], f)
            d.append(now - prev)
        even, odd = d[0] + d[2], d[1] + d[3]
        x0 = dot3(even + odd, *a)
        y0 = dot3(even - odd, *b)
        w = dot3(jnp.concatenate([d[0] - d[2], d[1] - d[3]], axis=1), *r)
        p, q = x0 + y0, x0 - y0
        outs[0][c] = p + w[:, :256]
        outs[1][c] = q + w[:, 256:]
        outs[2][c] = p - w[:, :256]
        outs[3][c] = q - w[:, 256:]


def weight_call(half, t, f, rows, x, own, extra, come):
    pieces = [*own, *extra, *(come if half == 0 else ())]
    return call(
        functools.partial(weight_kernel, half),
        [array(3, CHUNK, 256)] * 4,
        [smem_spec()] + [vmem_spec()] * 4 + [hbm_spec()] + [vmem_spec()] * len(pieces),
        [vmem_spec()] * 4,
        [pltpu.VMEM((3, CHUNK, 256), F32), dma_sems(1)],
        10,
    )(t, f, *rows, x, *pieces)


def coriolis_rows(total, first, offsets):
    index = (first + offsets).astype(F32)
    return 2.0 * coriolis_peak * jnp.sin(2.0 * jnp.pi * (index + 0.5) / total)


def ring(count, shift):
    return [(i, (i + shift) % count) for i in range(count)]


def to_next(value, j):
    pairs = [
        (s * LON + a, ((s + 1) % SUB) * LON + (a + j) % LON)
        for s in range(SUB)
        for a in range(LON)
    ]
    return lax.ppermute(value, ("sub", "lon"), pairs)


def to_lon(value, j):
    return lax.ppermute(value, "lon", ring(LON, j))


ORDER = (0, 3, 2, 1)


def shards(segment_launch_values, initial_backdrop, spectral_inverse_variances):
    x = segment_launch_values[0]
    sub, lat, lon = (lax.axis_index(n) for n in ("sub", "lat", "lon"))
    tile_rows = x.shape[1]
    total = tile_rows * lax.axis_size("lat")
    i = jnp.arange(2 * LON + 1, dtype=jnp.int32)
    t = lax.rem(jnp.where(i < LON, lon + i, lon - i + 2 * LON), LON)
    t = jnp.where(i < 2 * LON, t, sub)

    above = lax.ppermute(x[:, tile_rows - 16 :], "lat", ring(8, 1))
    below = lax.ppermute(x[:, :16], "lat", ring(8, -1))
    sent, blocks = rows_to_send(t, x, initial_backdrop)
    extra = {}
    for j, block in zip((2, 1, 3, 0), blocks):
        pairs = [(s * LON + a, s * LON + (a + j) % LON) for s in (0, SUB - 1) for a in range(LON)]
        extra[j] = lax.ppermute(block, ("sub", "lon"), pairs) if j else block
    extra = [extra[j] for j in (0, 3, 2, 1)]
    sent = add_edges(t, x, above, below, sent)
    s2, s1, s3, s0 = (to_next(v, j) for v, j in zip(sent, (2, 1, 3, 0)))
    come = [s0, s3, s2, s1]

    s0, variances = lax.optimization_barrier((s0, spectral_inverse_variances))
    first_row = lat * tile_rows + lon * ROWS
    offsets = jnp.arange(TILES + SPARE) - HALO
    f1 = coriolis_rows(total, first_row, offsets)
    f2 = coriolis_rows(total, first_row, offsets + CHUNK)
    rows = weighting_rows(variances)
    s3, *tied = lax.optimization_barrier((s3, *rows, *extra))
    rows, extra = tied[:3], tied[3:]
    own = [lax.ppermute(v, "sub", ring(SUB, -1)) for v in (s3, s2, s1)]

    m1 = model_call(False, f1, come)
    o1 = weight_call(0, t, m1, rows, x, own, extra, come)
    r1 = [to_lon(o1[j], j) if j else o1[j] for j in range(LON)]
    f2, *o1 = lax.optimization_barrier((f2, *o1))
    m2 = model_call(True, f2, come)
    o2 = weight_call(1, t, m2, rows, x, own, extra, come)
    r2 = [to_lon(o2[j], j) if j else o2[j] for j in range(LON)]
    return place(t, r2, tile_rows, place(t, r1, tile_rows))[None]


def solution(mesh):
    return jax.shard_map(
        shards,
        mesh=mesh,
        in_specs=(P("sub", None, "lat", "lon"), P(None, "lat", "lon"), P()),
        out_specs=P("sub", None, "lat", "lon"),
        check_vma=False,
    )
```

```python
import functools

import numpy as np
import jax
import jax.numpy as jnp
from jax import lax
from jax.experimental import pallas as pl
from jax.experimental.pallas import tpu as pltpu
from jax.sharding import PartitionSpec as P

NLON = 1024
STEPS = 3
time_step = 0.5
coriolis_peak = 0.4

SUB = 8
LON = 4
ROWS = 128
HALO = 3 * STEPS
CHUNK = ROWS // 2
SENT = 440
TILES = CHUNK + 2 * HALO
GROUP = 16
SPARE = 2 * GROUP
F32 = jnp.float32
BF16 = jnp.bfloat16


def vmem_spec():
    return pl.BlockSpec(memory_space=pltpu.VMEM)


def smem_spec():
    return pl.BlockSpec(memory_space=pltpu.SMEM)


def hbm_spec():
    return pl.BlockSpec(memory_space=pltpu.HBM)


def call(kernel, outs, in_specs, out_specs, scratch, mib, **kwargs):
    return pl.pallas_call(
        kernel,
        out_shape=outs,
        in_specs=in_specs,
        out_specs=out_specs,
        scratch_shapes=scratch,
        compiler_params=pltpu.CompilerParams(vmem_limit_bytes=mib << 20),
        cost_estimate=pl.CostEstimate(flops=0, bytes_accessed=1, transcendentals=0),
        **kwargs,
    )


def array(*shape):
    return jax.ShapeDtypeStruct(shape, F32)


def dma_sems(n):
    return pltpu.SemaphoreType.DMA((n,))


def start_all(sem, pairs):
    copies = [pltpu.make_async_copy(a, b, sem.at[n]) for n, (a, b) in enumerate(pairs)]
    for copy in copies:
        copy.start()
    return copies


def aligned(row):
    return pl.multiple_of(row, 16)


def unpack_rows(dst, piece, field, first, count, row0, block):
    done = 0
    while done < count:
        n = min(8, count - done)
        for half in range(2):
            value = piece[first + done : first + done + n, 128 * half : 128 * half + 128]
            start = (row0 + done) * 8 + 2 * block + half
            where = pl.ds(start, n, stride=8) if n > 1 else pl.ds(start, 1)
            dst[field, where, :] = value + 1.0 if field == 0 else value
        done += n


def stage(src, base, dst, f_ref, lo, rows, kind):
    lane = lax.broadcasted_iota(jnp.int32, (8, 128), 1)
    is_first = lane == 0
    is_last = lane == 127

    def neighbours(a):
        up = pltpu.roll(a, 127, 1)
        down = pltpu.roll(a, 1, 1)
        up = jnp.where(is_last, pltpu.roll(up, 7, 0), up)
        down = jnp.where(is_first, pltpu.roll(down, 1, 0), down)
        return up, down

    def body(g, carry):
        row = lo + g * GROUP

        def load(ref, c, k):
            return ref[c, pl.ds(pl.multiple_of((row + k) * 8, 8), 8), :]

        d = [load(src, 0, k) for k in range(-1, GROUP + 1)]
        u = [load(src, 1, k) for k in range(-1, GROUP + 1)]
        v = [load(src, 2, k) for k in range(-1, GROUP + 1)]
        flux = [d[k] * v[k] for k in range(GROUP + 2)]
        for k in range(1, GROUP + 1):
            f = f_ref[row + k - 1]
            d_up, d_down = neighbours(d[k])
            u_up, u_down = neighbours(u[k])
            v_up, v_down = neighbours(v[k])
            t_h = (d_up * u_up - d_down * u_down) + (flux[k + 1] - flux[k - 1])
            t_u = u[k] * (u_up - u_down) + v[k] * ((u[k + 1] - u[k - 1]) - f) + (d_up - d_down)
            t_v = u[k] * ((v_up - v_down) + f) + v[k] * (v[k + 1] - v[k - 1]) + (d[k + 1] - d[k - 1])
            for c, (now, t) in enumerate(((d[k], t_h), (u[k], t_u), (v[k], t_v))):
                new = now - (0.5 * time_step) * t
                if kind == 1:
                    new = 0.75 * load(base, c, k - 1) + 0.25 * new
                elif kind == 2:
                    new = (1.0 / 3.0) * load(base, c, k - 1) + (2.0 / 3.0) * new
                dst[c, pl.ds(pl.multiple_of((row + k - 1) * 8, 8), 8), :] = new
        return carry

    lax.fori_loop(0, -(-rows // GROUP), body, 0)


def half_of(chunk, t_ref):
    swapped = jnp.where(t_ref[2 * LON] == SUB - 1, 1, 0)
    return 1 - swapped if chunk else swapped


def model_kernel(chunk, t_ref, f_ref, s0, s3, s2, s1, out, *bufs):
    x, b, c, y = bufs
    half = half_of(chunk, t_ref)

    def unpack(second):
        for block, s in enumerate((s0, s3, s2, s1)):
            for field in range(3):
                row = ROWS * field
                edge = 3 * ROWS + 2 * HALO * field
                if second:
                    unpack_rows(x, s, field, row + CHUNK - HALO, 1, 0, block)
                    unpack_rows(x, s, field, row + CHUNK - HALO + 1, CHUNK + HALO - 1, 1, block)
                    unpack_rows(x, s, field, edge + HALO, HALO, CHUNK + HALO, block)
                else:
                    unpack_rows(x, s, field, edge, HALO, 0, block)
                    unpack_rows(x, s, field, row, CHUNK + HALO, HALO, block)

    @pl.when(half == 0)
    def _():
        unpack(False)

    @pl.when(half == 1)
    def _():
        unpack(True)

    done = 0
    for _ in range(STEPS):
        for kind, (src, base, dst) in enumerate(((x, x, b), (b, x, c), (c, x, y))):
            done += 1
            stage(src, base, dst, f_ref, done, TILES - 2 * done, kind)
        x, y = y, x
    for field in range(3):
        for r in range(0, CHUNK, 8):
            for s in range(8):
                value = x[field, pl.ds((HALO + r) * 8 + s, 8, stride=8), :]
                out[field, r : r + 8, 128 * s : 128 * s + 128] = (
                    value - 1.0 if field == 0 else value
                )


def model_call(chunk, t, f, pieces):
    return call(
        functools.partial(model_kernel, chunk),
        array(3, CHUNK, NLON),
        [smem_spec()] * 2 + [vmem_spec()] * 4,
        vmem_spec(),
        [pltpu.VMEM((3, (TILES + SPARE) * 8, 128), F32)] * 4,
        10,
    )(t, f, *pieces)


def rows_kernel(t_ref, x, back, s2, s1, s3, s0, e2, e1, e3, e0, sem, sem_extra):
    order = ((2, s2, e2), (1, s1, e1), (3, s3, e3), (0, s0, e0))
    at = [aligned(t_ref[j] * ROWS) for j, _, _ in order]
    pairs = []
    for row, (_, s, _) in zip(at, order):
        for c in range(3):
            pairs.append((x.at[c, pl.ds(row, ROWS), :], s.at[pl.ds(ROWS * c, ROWS), :]))
    copies = start_all(sem, pairs)

    @pl.when(t_ref[2 * LON] == 0)
    def _():
        pairs = [
            (back.at[:, pl.ds(aligned(row + CHUNK), CHUNK), :], e)
            for row, (_, _, e) in zip(at, order)
        ]
        for copy in start_all(sem_extra, pairs):
            copy.wait()

    @pl.when(t_ref[2 * LON] == SUB - 1)
    def _():
        pairs = [(x.at[:, pl.ds(row, CHUNK), :], e) for row, (_, _, e) in zip(at, order)]
        for copy in start_all(sem_extra, pairs):
            copy.wait()

    for copy in copies:
        copy.wait()

    @pl.when(t_ref[2 * LON] == SUB - 1)
    def _():
        pairs = []
        for row, (_, s, _) in zip(at, order):
            for c in range(3):
                pairs.append((back.at[c, pl.ds(row, CHUNK), :], s.at[pl.ds(ROWS * c, CHUNK), :]))
        for copy in start_all(sem, pairs):
            copy.wait()

    for _, s, _ in order:
        s[3 * ROWS :, :] = jnp.zeros((SENT - 3 * ROWS, 256), F32)


def rows_to_send(t, x, back):
    out = call(
        rows_kernel,
        [array(SENT, 256)] * 4 + [array(3, CHUNK, 256)] * 4,
        [smem_spec(), hbm_spec(), hbm_spec()],
        [vmem_spec()] * 8,
        [dma_sems(12), dma_sems(4)],
        60,
    )(t, x, back)
    return out[:4], out[4:]


def edges_kernel(t_ref, x, above, below, *refs):
    outs = refs[4:8]
    edges, ready, sem, sem_out = refs[8:]
    rows = x.shape[1]
    pairs = []
    for q in range(1, LON):
        pairs.append((x.at[:, pl.ds(ROWS * q - 16, 32), :], edges.at[q]))
    pairs += [
        (x.at[:, pl.ds(0, 16), :], edges.at[0, :, pl.ds(16, 16), :]),
        (above, edges.at[0, :, pl.ds(0, 16), :]),
        (x.at[:, pl.ds(rows - 16, 16), :], edges.at[LON, :, pl.ds(0, 16), :]),
        (below, edges.at[LON, :, pl.ds(16, 16), :]),
    ]
    for copy in start_all(sem, pairs):
        copy.wait()
    pairs = []
    for n, j in enumerate((2, 1, 3, 0)):
        for c in range(3):
            edge = 2 * HALO * c
            ready[n, edge : edge + HALO, :] = edges[t_ref[j], c, 16 - HALO : 16, :]
            ready[n, edge + HALO : edge + 2 * HALO, :] = edges[t_ref[j] + 1, c, 16 : 16 + HALO, :]
        ready[n, 6 * HALO :, :] = jnp.zeros((SENT - 3 * ROWS - 6 * HALO, 256), F32)
        pairs.append((ready.at[n], outs[n].at[pl.ds(3 * ROWS, SENT - 3 * ROWS), :]))
    for copy in start_all(sem_out, pairs):
        copy.wait()


def add_edges(t, x, above, below, sent):
    return call(
        edges_kernel,
        [array(SENT, 256)] * 4,
        [smem_spec()] + [hbm_spec()] * 7,
        [hbm_spec()] * 4,
        [
            pltpu.VMEM((LON + 1, 3, 32, 256), F32),
            pltpu.VMEM((4, SENT - 3 * ROWS, 256), F32),
            dma_sems(7),
            dma_sems(4),
        ],
        60,
        input_output_aliases={4: 0, 5: 1, 6: 2, 7: 3},
    )(t, x, above, below, *sent)


def place_kernel(chunk, t_ref, o0, r1, r2, r3, *refs):
    out, buf, sem, sem_out = refs[-4:]
    first = CHUNK * half_of(chunk, t_ref)
    copies = start_all(sem, [(r, buf.at[j]) for j, r in enumerate((o0, r1, r2, r3))])
    outs = []
    for j, copy in enumerate(copies):
        copy.wait()
        where = out.at[:, pl.ds(aligned(t_ref[LON + j] * ROWS + first), CHUNK), :]
        outs.append(pltpu.make_async_copy(buf.at[j], where, sem_out.at[j]))
        outs[-1].start()
    for copy in outs:
        copy.wait()


def place(t, pieces, rows, begun=None):
    extra = [] if begun is None else [begun]
    return call(
        functools.partial(place_kernel, 1 if extra else 0),
        [array(3, rows, 256)],
        [smem_spec()] + [hbm_spec()] * (4 + len(extra)),
        [hbm_spec()],
        [pltpu.VMEM((4, 3, CHUNK, 256), F32), dma_sems(4), dma_sems(4)],
        3,
        input_output_aliases={5: 0} if extra else {},
    )(t, *pieces, *extra)[0]


def cosine_table():
    m = np.arange(NLON // 2 + 1)
    n = np.arange(NLON)
    factor = np.where((m == 0) | (m == NLON // 2), 1.0, 2.0) / NLON
    angle = 2.0 * np.pi / NLON * ((m[:, None] * n[None, :]) % NLON)
    return (factor[:, None] * np.cos(angle)).astype(np.float32)


def split(x):
    high = x.astype(BF16)
    return high, (x - high.astype(F32)).astype(BF16)


def toeplitz(row, size, sign):
    full = pltpu.roll(jnp.broadcast_to(row, (size, size)), 0, 1, stride=1, stride_axis=0)
    if sign < 0:
        c = lax.broadcasted_iota(jnp.int32, (size, size), 0)
        r = lax.broadcasted_iota(jnp.int32, (size, size), 1)
        full = jnp.where(r < c, -full, full)
    return full


def weighting_rows(variances):
    k = jnp.dot(variances, jnp.asarray(cosine_table()), precision=lax.Precision.HIGHEST)
    k0, k1, k2, k3 = (k[:, 256 * j : 256 * j + 256] for j in range(4))
    even = (k0 + k2) * 0.25
    odd = (k1 + k3) * 0.25
    return even + odd, even - odd, (k[:, :512] - k[:, 512:]) * 0.5


def dot3(x, high, low):
    n = x.shape[0]
    xh, xl = split(x)
    y = jnp.dot(jnp.concatenate([xh, xl], axis=0), high, preferred_element_type=F32)
    return y[:n] + y[n:] + jnp.dot(xh, low, preferred_element_type=F32)


def weight_kernel(chunk, t_ref, f_ref, a_ref, b_ref, r_ref, *refs):
    own, other, outs = refs[:4], refs[4:8], refs[8:]
    half = half_of(chunk, t_ref)
    first = t_ref[2 * LON] == 0
    last = t_ref[2 * LON] == SUB - 1
    for c in range(3):
        a = split(toeplitz(a_ref[c : c + 1, :], 256, 1))
        b = split(toeplitz(b_ref[c : c + 1, :], 256, -1))
        r = split(toeplitz(r_ref[c : c + 1, :], 512, -1))
        d = []
        rows = pl.ds(pl.multiple_of(ROWS * c + CHUNK * half, CHUNK), CHUNK)
        for block in range(4):
            f = f_ref[c, :, 256 * block : 256 * block + 256]
            now = own[block][rows, :]
            if chunk == 0:
                prev = jnp.where(first, other[block][rows, :], f)
            else:
                now = jnp.where(last, other[block][c], now)
                prev = jnp.where(first, other[block][c], f)
            d.append(now - prev)
        even, odd = d[0] + d[2], d[1] + d[3]
        x0 = dot3(even + odd, *a)
        y0 = dot3(even - odd, *b)
        w = dot3(jnp.concatenate([d[0] - d[2], d[1] - d[3]], axis=1), *r)
        p, q = x0 + y0, x0 - y0
        outs[0][c] = p + w[:, :256]
        outs[1][c] = q + w[:, 256:]
        outs[2][c] = p - w[:, :256]
        outs[3][c] = q - w[:, 256:]


def weight_call(chunk, t, f, rows, own, other):
    pieces = [*own, *other]
    return call(
        functools.partial(weight_kernel, chunk),
        [array(3, CHUNK, 256)] * 4,
        [smem_spec()] + [vmem_spec()] * 4 + [vmem_spec()] * len(pieces),
        [vmem_spec()] * 4,
        [],
        10,
    )(t, f, *rows, *pieces)


def coriolis_rows(total, first, offsets):
    index = (first + offsets).astype(F32)
    return 2.0 * coriolis_peak * jnp.sin(2.0 * jnp.pi * (index + 0.5) / total)


def ring(count, shift):
    return [(i, (i + shift) % count) for i in range(count)]


def to_next(value, j):
    pairs = [
        (s * LON + a, ((s + 1) % SUB) * LON + (a + j) % LON)
        for s in range(SUB)
        for a in range(LON)
    ]
    return lax.ppermute(value, ("sub", "lon"), pairs)


def to_lon(value, j):
    return lax.ppermute(value, "lon", ring(LON, j))


ORDER = (0, 3, 2, 1)


def shards(segment_launch_values, initial_backdrop, spectral_inverse_variances):
    x = segment_launch_values[0]
    sub, lat, lon = (lax.axis_index(n) for n in ("sub", "lat", "lon"))
    tile_rows = x.shape[1]
    total = tile_rows * lax.axis_size("lat")
    i = jnp.arange(2 * LON + 1, dtype=jnp.int32)
    t = lax.rem(jnp.where(i < LON, lon + i, lon - i + 2 * LON), LON)
    t = jnp.where(i < 2 * LON, t, sub)

    above = lax.ppermute(x[:, tile_rows - 16 :], "lat", ring(8, 1))
    below = lax.ppermute(x[:, :16], "lat", ring(8, -1))
    sent, blocks = rows_to_send(t, x, initial_backdrop)
    sent = add_edges(t, x, above, below, sent)
    s2, s1, s3, s0 = (to_next(v, j) for v, j in zip(sent, (2, 1, 3, 0)))
    come = [s0, s3, s2, s1]

    s0, variances, *blocks = lax.optimization_barrier((s0, spectral_inverse_variances, *blocks))
    first_row = lat * tile_rows + lon * ROWS
    offsets = jnp.arange(TILES + SPARE) - HALO
    swapped = jnp.where(sub == SUB - 1, CHUNK, 0)
    f1 = coriolis_rows(total, first_row + swapped, offsets)
    f2 = coriolis_rows(total, first_row - swapped, offsets + CHUNK)
    rows = weighting_rows(variances)
    extra = {}
    for j, block in zip((2, 1, 3, 0), blocks):
        pairs = [(s * LON + a, s * LON + (a + j) % LON) for s in (0, SUB - 1) for a in range(LON)]
        extra[j] = lax.ppermute(block, ("sub", "lon"), pairs) if j else block
    extra = [extra[j] for j in (0, 3, 2, 1)]
    s3, *rows = lax.optimization_barrier((s3, *rows))
    own = [sent[3]] + [lax.ppermute(v, "sub", ring(SUB, -1)) for v in (s3, s2, s1)]

    m1 = model_call(0, t, f1, come)
    o1 = weight_call(0, t, m1, rows, own, come)
    r1 = [to_lon(o1[j], j) if j else o1[j] for j in range(LON)]
    f2, *tied = lax.optimization_barrier((f2, *o1, *extra))
    o1, extra = tied[:LON], tied[LON:]
    m2 = model_call(1, t, f2, come)
    o2 = weight_call(1, t, m2, rows, own, extra)
    r2 = [to_lon(o2[j], j) if j else o2[j] for j in range(LON)]
    return place(t, r2, tile_rows, place(t, r1, tile_rows))[None]


def solution(mesh):
    return jax.shard_map(
        shards,
        mesh=mesh,
        in_specs=(P("sub", None, "lat", "lon"), P(None, "lat", "lon"), P()),
        out_specs=P("sub", None, "lat", "lon"),
        check_vma=False,
    )
```

```python
import functools

import numpy as np
import jax
import jax.numpy as jnp
from jax import lax
from jax.experimental import pallas as pl
from jax.experimental.pallas import tpu as pltpu
from jax.sharding import PartitionSpec as P

NLON = 1024
STEPS = 3
time_step = 0.5
coriolis_peak = 0.4

SUB = 8
LON = 4
ROWS = 128
HALO = 3 * STEPS
CHUNK = ROWS // 2
SENT = 440
TILES = CHUNK + 2 * HALO
GROUP = 40
SPARE = 16
F32 = jnp.float32
BF16 = jnp.bfloat16


def vmem_spec():
    return pl.BlockSpec(memory_space=pltpu.VMEM)


def smem_spec():
    return pl.BlockSpec(memory_space=pltpu.SMEM)


def hbm_spec():
    return pl.BlockSpec(memory_space=pltpu.HBM)


def call(kernel, outs, in_specs, out_specs, scratch, mib, **kwargs):
    return pl.pallas_call(
        kernel,
        out_shape=outs,
        in_specs=in_specs,
        out_specs=out_specs,
        scratch_shapes=scratch,
        compiler_params=pltpu.CompilerParams(vmem_limit_bytes=mib << 20),
        cost_estimate=pl.CostEstimate(flops=0, bytes_accessed=1, transcendentals=0),
        **kwargs,
    )


def array(*shape):
    return jax.ShapeDtypeStruct(shape, F32)


def dma_sems(n):
    return pltpu.SemaphoreType.DMA((n,))


def start_all(sem, pairs):
    copies = [pltpu.make_async_copy(a, b, sem.at[n]) for n, (a, b) in enumerate(pairs)]
    for copy in copies:
        copy.start()
    return copies


def aligned(row):
    return pl.multiple_of(row, 16)


def unpack_rows(dst, piece, field, first, count, row0, block):
    done = 0
    while done < count:
        n = min(8, count - done)
        for half in range(2):
            value = piece[first + done : first + done + n, 128 * half : 128 * half + 128]
            start = (row0 + done) * 8 + 2 * block + half
            where = pl.ds(start, n, stride=8) if n > 1 else pl.ds(start, 1)
            dst[field, where, :] = value + 1.0 if field == 0 else value
        done += n


def stage(src, base, dst, f_ref, lo, rows, kind):
    lane = lax.broadcasted_iota(jnp.int32, (8, 128), 1)
    is_first = lane == 0
    is_last = lane == 127

    def neighbours(a):
        up = pltpu.roll(a, 127, 1)
        down = pltpu.roll(a, 1, 1)
        up = jnp.where(is_last, pltpu.roll(up, 7, 0), up)
        down = jnp.where(is_first, pltpu.roll(down, 1, 0), down)
        return up, down

    def body(g, carry):
        row = lo + g * GROUP

        def load(ref, c, k):
            return ref[c, pl.ds(pl.multiple_of((row + k) * 8, 8), 8), :]

        d = [load(src, 0, k) for k in range(-1, GROUP + 1)]
        u = [load(src, 1, k) for k in range(-1, GROUP + 1)]
        v = [load(src, 2, k) for k in range(-1, GROUP + 1)]
        flux = [d[k] * v[k] for k in range(GROUP + 2)]
        for k in range(1, GROUP + 1):
            f = f_ref[row + k - 1]
            d_up, d_down = neighbours(d[k])
            u_up, u_down = neighbours(u[k])
            v_up, v_down = neighbours(v[k])
            t_h = (d_up * u_up - d_down * u_down) + (flux[k + 1] - flux[k - 1])
            t_u = u[k] * (u_up - u_down) + v[k] * ((u[k + 1] - u[k - 1]) - f) + (d_up - d_down)
            t_v = u[k] * ((v_up - v_down) + f) + v[k] * (v[k + 1] - v[k - 1]) + (d[k + 1] - d[k - 1])
            for c, (now, t) in enumerate(((d[k], t_h), (u[k], t_u), (v[k], t_v))):
                new = now - (0.5 * time_step) * t
                if kind == 1:
                    new = 0.75 * load(base, c, k - 1) + 0.25 * new
                elif kind == 2:
                    new = (1.0 / 3.0) * load(base, c, k - 1) + (2.0 / 3.0) * new
                dst[c, pl.ds(pl.multiple_of((row + k - 1) * 8, 8), 8), :] = new
        return carry

    lax.fori_loop(0, -(-rows // GROUP), body, 0)


def half_of(chunk, t_ref):
    swapped = jnp.where(t_ref[2 * LON] == SUB - 1, 1, 0)
    return 1 - swapped if chunk else swapped


def model_kernel(chunk, t_ref, f_ref, s0, s3, s2, s1, out, *bufs):
    x, b, c, y = bufs
    half = half_of(chunk, t_ref)

    def unpack(second):
        for block, s in enumerate((s0, s3, s2, s1)):
            for field in range(3):
                row = ROWS * field
                edge = 3 * ROWS + 2 * HALO * field
                if second:
                    unpack_rows(x, s, field, row + CHUNK - HALO, 1, 0, block)
                    unpack_rows(x, s, field, row + CHUNK - HALO + 1, CHUNK + HALO - 1, 1, block)
                    unpack_rows(x, s, field, edge + HALO, HALO, CHUNK + HALO, block)
                else:
                    unpack_rows(x, s, field, edge, HALO, 0, block)
                    unpack_rows(x, s, field, row, CHUNK + HALO, HALO, block)

    @pl.when(half == 0)
    def _():
        unpack(False)

    @pl.when(half == 1)
    def _():
        unpack(True)

    done = 0
    for _ in range(STEPS):
        for kind, (src, base, dst) in enumerate(((x, x, b), (b, x, c), (c, x, y))):
            done += 1
            stage(src, base, dst, f_ref, done, TILES - 2 * done, kind)
        x, y = y, x
    for field in range(3):
        for r in range(0, CHUNK, 8):
            for s in range(8):
                value = x[field, pl.ds((HALO + r) * 8 + s, 8, stride=8), :]
                out[field, r : r + 8, 128 * s : 128 * s + 128] = (
                    value - 1.0 if field == 0 else value
                )


def model_call(chunk, t, f, pieces):
    return call(
        functools.partial(model_kernel, chunk),
        array(3, CHUNK, NLON),
        [smem_spec()] * 2 + [vmem_spec()] * 4,
        vmem_spec(),
        [pltpu.VMEM((3, (TILES + SPARE) * 8, 128), F32)] * 4,
        10,
    )(t, f, *pieces)


def extra_kernel(t_ref, x, back, e2, e1, e3, e0, buf, sem, sem_out):
    order = ((2, e2), (1, e1), (3, e3), (0, e0))
    at = [aligned(t_ref[j] * ROWS) for j, _ in order]

    def move(src, first):
        pairs = [
            (src.at[:, pl.ds(aligned(row + first), CHUNK), :], buf.at[n])
            for n, row in enumerate(at)
        ]
        for copy in start_all(sem, pairs):
            copy.wait()
        for copy in start_all(sem_out, [(buf.at[n], e) for n, (_, e) in enumerate(order)]):
            copy.wait()

    @pl.when(t_ref[2 * LON] == 0)
    def _():
        move(back, CHUNK)

    @pl.when(t_ref[2 * LON] == SUB - 1)
    def _():
        move(x, 0)


def extra_rows(t, x, back):
    return call(
        extra_kernel,
        [array(3, CHUNK, 256)] * 4,
        [smem_spec(), hbm_spec(), hbm_spec()],
        [hbm_spec()] * 4,
        [pltpu.VMEM((4, 3, CHUNK, 256), F32), dma_sems(4), dma_sems(4)],
        60,
    )(t, x, back)


def rows_kernel(t_ref, x, back, s2, s1, s3, s0, buf, sem, sem_out):
    order = ((2, s2), (1, s1), (3, s3), (0, s0))
    at = [aligned(t_ref[j] * ROWS) for j, _ in order]
    last = t_ref[2 * LON] == SUB - 1

    def move(parts):
        pairs = []
        for n, row in enumerate(at):
            for src, first, count in parts:
                for c in range(3):
                    dst = buf.at[n, pl.ds(ROWS * c + first, count), :]
                    pairs.append((src.at[c, pl.ds(aligned(row + first), count), :], dst))
        copies = start_all(sem, pairs)
        each = 3 * len(parts)
        outs = []
        for n, (_, s) in enumerate(order):
            for copy in copies[each * n : each * n + each]:
                copy.wait()
            buf[n, 3 * ROWS :, :] = jnp.zeros((SENT - 3 * ROWS, 256), F32)
            outs.append(pltpu.make_async_copy(buf.at[n], s, sem_out.at[n]))
            outs[-1].start()
        for copy in outs:
            copy.wait()

    @pl.when(last)
    def _():
        move(((back, 0, CHUNK), (x, CHUNK, CHUNK)))

    @pl.when(jnp.logical_not(last))
    def _():
        move(((x, 0, ROWS),))


def rows_to_send(t, x, back):
    return call(
        rows_kernel,
        [array(SENT, 256)] * 4,
        [smem_spec(), hbm_spec(), hbm_spec()],
        [hbm_spec()] * 4,
        [pltpu.VMEM((4, SENT, 256), F32), dma_sems(24), dma_sems(4)],
        60,
    )(t, x, back)


def edges_kernel(t_ref, x, above, below, *refs):
    outs = refs[4:8]
    edges, ready, sem, sem_out = refs[8:]
    rows = x.shape[1]
    pairs = []
    for q in range(1, LON):
        pairs.append((x.at[:, pl.ds(ROWS * q - 16, 32), :], edges.at[q]))
    pairs += [
        (x.at[:, pl.ds(0, 16), :], edges.at[0, :, pl.ds(16, 16), :]),
        (above, edges.at[0, :, pl.ds(0, 16), :]),
        (x.at[:, pl.ds(rows - 16, 16), :], edges.at[LON, :, pl.ds(0, 16), :]),
        (below, edges.at[LON, :, pl.ds(16, 16), :]),
    ]
    for copy in start_all(sem, pairs):
        copy.wait()
    pairs = []
    for n, j in enumerate((2, 1, 3, 0)):
        for c in range(3):
            edge = 2 * HALO * c
            ready[n, edge : edge + HALO, :] = edges[t_ref[j], c, 16 - HALO : 16, :]
            ready[n, edge + HALO : edge + 2 * HALO, :] = edges[t_ref[j] + 1, c, 16 : 16 + HALO, :]
        ready[n, 6 * HALO :, :] = jnp.zeros((SENT - 3 * ROWS - 6 * HALO, 256), F32)
        pairs.append((ready.at[n], outs[n].at[pl.ds(3 * ROWS, SENT - 3 * ROWS), :]))
    for copy in start_all(sem_out, pairs):
        copy.wait()


def add_edges(t, x, above, below, sent):
    return call(
        edges_kernel,
        [array(SENT, 256)] * 4,
        [smem_spec()] + [hbm_spec()] * 7,
        [hbm_spec()] * 4,
        [
            pltpu.VMEM((LON + 1, 3, 32, 256), F32),
            pltpu.VMEM((4, SENT - 3 * ROWS, 256), F32),
            dma_sems(7),
            dma_sems(4),
        ],
        60,
        input_output_aliases={4: 0, 5: 1, 6: 2, 7: 3},
    )(t, x, above, below, *sent)


def place_first_kernel(t_ref, o0, r1, r2, r3, out, buf, sem, sem_out):
    first = CHUNK * half_of(0, t_ref)
    copies = start_all(sem, [(r, buf.at[j]) for j, r in enumerate((o0, r1, r2, r3))])
    outs = []
    for j, copy in enumerate(copies):
        copy.wait()
        where = out.at[:, pl.ds(aligned(t_ref[LON + j] * ROWS + first), CHUNK), :]
        outs.append(pltpu.make_async_copy(buf.at[j], where, sem_out.at[j]))
        outs[-1].start()
    for copy in outs:
        copy.wait()


def place_first(t, pieces, rows):
    return call(
        place_first_kernel,
        [array(3, rows, 256)],
        [smem_spec()] + [hbm_spec()] * 4,
        [hbm_spec()],
        [pltpu.VMEM((4, 3, CHUNK, 256), F32), dma_sems(4), dma_sems(4)],
        4,
    )(t, *pieces)[0]


def place_second_kernel(t_ref, o0, r1, r2, r3, begun, out, sem):
    first = CHUNK * half_of(1, t_ref)
    pairs = [
        (r, out.at[:, pl.ds(aligned(t_ref[LON + j] * ROWS + first), CHUNK), :])
        for j, r in enumerate((o0, r1, r2, r3))
    ]
    for copy in start_all(sem, pairs):
        copy.wait()


def place_second(t, pieces, begun):
    return call(
        place_second_kernel,
        [array(*begun.shape)],
        [smem_spec()] + [vmem_spec()] * 4 + [hbm_spec()],
        [hbm_spec()],
        [dma_sems(4)],
        4,
        input_output_aliases={5: 0},
    )(t, *pieces, begun)[0]


def cosine_table():
    m = np.arange(NLON // 2 + 1)
    n = np.arange(NLON)
    factor = np.where((m == 0) | (m == NLON // 2), 1.0, 2.0) / NLON
    angle = 2.0 * np.pi / NLON * ((m[:, None] * n[None, :]) % NLON)
    return (factor[:, None] * np.cos(angle)).astype(np.float32)


def split(x):
    high = x.astype(BF16)
    return high, (x - high.astype(F32)).astype(BF16)


def toeplitz(row, size, sign):
    full = pltpu.roll(jnp.broadcast_to(row, (size, size)), 0, 1, stride=1, stride_axis=0)
    if sign < 0:
        c = lax.broadcasted_iota(jnp.int32, (size, size), 0)
        r = lax.broadcasted_iota(jnp.int32, (size, size), 1)
        full = jnp.where(r < c, -full, full)
    return full


def weighting_rows(variances):
    k = jnp.dot(variances, jnp.asarray(cosine_table()), precision=lax.Precision.HIGHEST)
    k0, k1, k2, k3 = (k[:, 256 * j : 256 * j + 256] for j in range(4))
    even = (k0 + k2) * 0.25
    odd = (k1 + k3) * 0.25
    return even + odd, even - odd, (k[:, :512] - k[:, 512:]) * 0.5


def dot3(x, high, low):
    n = x.shape[0]
    xh, xl = split(x)
    y = jnp.dot(jnp.concatenate([xh, xl], axis=0), high, preferred_element_type=F32)
    return y[:n] + y[n:] + jnp.dot(xh, low, preferred_element_type=F32)


def weight_kernel(chunk, t_ref, f_ref, a_ref, b_ref, r_ref, *refs):
    own, other, outs = refs[:4], refs[4:8], refs[8:]
    half = half_of(chunk, t_ref)
    first = t_ref[2 * LON] == 0
    last = t_ref[2 * LON] == SUB - 1
    for c in range(3):
        a = split(toeplitz(a_ref[c : c + 1, :], 256, 1))
        b = split(toeplitz(b_ref[c : c + 1, :], 256, -1))
        r = split(toeplitz(r_ref[c : c + 1, :], 512, -1))
        d = []
        rows = pl.ds(pl.multiple_of(ROWS * c + CHUNK * half, CHUNK), CHUNK)
        for block in range(4):
            f = f_ref[c, :, 256 * block : 256 * block + 256]
            now = own[block][rows, :]
            if chunk == 0:
                prev = jnp.where(first, other[block][rows, :], f)
            else:
                now = jnp.where(last, other[block][c], now)
                prev = jnp.where(first, other[block][c], f)
            d.append(now - prev)
        even, odd = d[0] + d[2], d[1] + d[3]
        x0 = dot3(even + odd, *a)
        y0 = dot3(even - odd, *b)
        w = dot3(jnp.concatenate([d[0] - d[2], d[1] - d[3]], axis=1), *r)
        p, q = x0 + y0, x0 - y0
        outs[0][c] = p + w[:, :256]
        outs[1][c] = q + w[:, 256:]
        outs[2][c] = p - w[:, :256]
        outs[3][c] = q - w[:, 256:]


def weight_call(chunk, t, f, rows, own, other):
    pieces = [*own, *other]
    return call(
        functools.partial(weight_kernel, chunk),
        [array(3, CHUNK, 256)] * 4,
        [smem_spec()] + [vmem_spec()] * 4 + [vmem_spec()] * len(pieces),
        [vmem_spec()] * 4,
        [],
        10,
    )(t, f, *rows, *pieces)


def coriolis_rows(total, first, offsets):
    index = (first + offsets).astype(F32)
    return 2.0 * coriolis_peak * jnp.sin(2.0 * jnp.pi * (index + 0.5) / total)


def ring(count, shift):
    return [(i, (i + shift) % count) for i in range(count)]


def to_next(value, j):
    pairs = [
        (s * LON + a, ((s + 1) % SUB) * LON + (a + j) % LON)
        for s in range(SUB)
        for a in range(LON)
    ]
    return lax.ppermute(value, ("sub", "lon"), pairs)


def to_lon(value, j):
    return lax.ppermute(value, "lon", ring(LON, j))


ORDER = (0, 3, 2, 1)


def shards(segment_launch_values, initial_backdrop, spectral_inverse_variances):
    x = segment_launch_values[0]
    sub, lat, lon = (lax.axis_index(n) for n in ("sub", "lat", "lon"))
    tile_rows = x.shape[1]
    total = tile_rows * lax.axis_size("lat")
    i = jnp.arange(2 * LON + 1, dtype=jnp.int32)
    t = lax.rem(jnp.where(i < LON, lon + i, lon - i + 2 * LON), LON)
    t = jnp.where(i < 2 * LON, t, sub)

    above = lax.ppermute(x[:, tile_rows - 16 :], "lat", ring(8, 1))
    below = lax.ppermute(x[:, :16], "lat", ring(8, -1))
    sent = rows_to_send(t, x, initial_backdrop)
    sent = add_edges(t, x, above, below, sent)
    s2, s1, s3, s0 = (to_next(v, j) for v, j in zip(sent, (2, 1, 3, 0)))
    come = [s0, s3, s2, s1]

    s0, variances, later = lax.optimization_barrier((s0, spectral_inverse_variances, t))
    blocks = extra_rows(later, x, initial_backdrop)
    first_row = lat * tile_rows + lon * ROWS
    offsets = jnp.arange(TILES + SPARE) - HALO
    swapped = jnp.where(sub == SUB - 1, CHUNK, 0)
    f1 = coriolis_rows(total, first_row + swapped, offsets)
    f2 = coriolis_rows(total, first_row - swapped, offsets + CHUNK)
    rows = weighting_rows(variances)
    s3, *tied = lax.optimization_barrier((s3, *rows, *blocks))
    rows, blocks = tied[:3], tied[3:]
    extra = {}
    for j, block in zip((2, 1, 3, 0), blocks):
        pairs = [(s * LON + a, s * LON + (a + j) % LON) for s in (0, SUB - 1) for a in range(LON)]
        extra[j] = lax.ppermute(block, ("sub", "lon"), pairs) if j else block
    extra = [extra[j] for j in (0, 3, 2, 1)]
    own = [sent[3]] + [lax.ppermute(v, "sub", ring(SUB, -1)) for v in (s3, s2, s1)]

    m1 = model_call(0, t, f1, come)
    o1 = weight_call(0, t, m1, rows, own, come)
    r1 = [to_lon(o1[j], j) if j else o1[j] for j in range(LON)]
    f2, *tied = lax.optimization_barrier((f2, *o1, *extra))
    o1, extra = tied[:LON], tied[LON:]
    m2 = model_call(1, t, f2, come)
    o2 = weight_call(1, t, m2, rows, own, extra)
    r2 = [to_lon(o2[j], j) if j else o2[j] for j in range(LON)]
    return place_second(t, r2, place_first(t, r1, tile_rows))[None]


def solution(mesh):
    return jax.shard_map(
        shards,
        mesh=mesh,
        in_specs=(P("sub", None, "lat", "lon"), P(None, "lat", "lon"), P()),
        out_specs=P("sub", None, "lat", "lon"),
        check_vma=False,
    )
```

```python
import functools

import numpy as np
import jax
import jax.numpy as jnp
from jax import lax
from jax.experimental import pallas as pl
from jax.experimental.pallas import tpu as pltpu
from jax.sharding import PartitionSpec as P

NLON = 1024
STEPS = 3
time_step = 0.5
coriolis_peak = 0.4

SUB = 8
LON = 4
ROWS = 128
HALO = 3 * STEPS
CHUNK = ROWS // 2
SENT = 440
TILES = CHUNK + 2 * HALO
GROUP = 40
SPARE = 16
F32 = jnp.float32
BF16 = jnp.bfloat16


def vmem_spec():
    return pl.BlockSpec(memory_space=pltpu.VMEM)


def smem_spec():
    return pl.BlockSpec(memory_space=pltpu.SMEM)


def hbm_spec():
    return pl.BlockSpec(memory_space=pltpu.HBM)


def call(kernel, outs, in_specs, out_specs, scratch, mib, **kwargs):
    return pl.pallas_call(
        kernel,
        out_shape=outs,
        in_specs=in_specs,
        out_specs=out_specs,
        scratch_shapes=scratch,
        compiler_params=pltpu.CompilerParams(vmem_limit_bytes=mib << 20),
        cost_estimate=pl.CostEstimate(flops=0, bytes_accessed=1, transcendentals=0),
        **kwargs,
    )


def array(*shape):
    return jax.ShapeDtypeStruct(shape, F32)


def dma_sems(n):
    return pltpu.SemaphoreType.DMA((n,))


def start_all(sem, pairs):
    copies = [pltpu.make_async_copy(a, b, sem.at[n]) for n, (a, b) in enumerate(pairs)]
    for copy in copies:
        copy.start()
    return copies


def aligned(row):
    return pl.multiple_of(row, 16)


def unpack_rows(dst, piece, field, first, count, row0, block):
    done = 0
    while done < count:
        n = min(8, count - done)
        for half in range(2):
            value = piece[first + done : first + done + n, 128 * half : 128 * half + 128]
            start = (row0 + done) * 8 + 2 * block + half
            where = pl.ds(start, n, stride=8) if n > 1 else pl.ds(start, 1)
            dst[field, where, :] = value + 1.0 if field == 0 else value
        done += n


def stage(src, base, dst, f_ref, lo, rows, kind):
    lane = lax.broadcasted_iota(jnp.int32, (8, 128), 1)
    is_first = lane == 0
    is_last = lane == 127

    def neighbours(a):
        up = pltpu.roll(a, 127, 1)
        down = pltpu.roll(a, 1, 1)
        up = jnp.where(is_last, pltpu.roll(up, 7, 0), up)
        down = jnp.where(is_first, pltpu.roll(down, 1, 0), down)
        return up, down

    def body(g, carry):
        row = lo + g * GROUP

        def load(ref, c, k):
            return ref[c, pl.ds(pl.multiple_of((row + k) * 8, 8), 8), :]

        d = [load(src, 0, k) for k in range(-1, GROUP + 1)]
        u = [load(src, 1, k) for k in range(-1, GROUP + 1)]
        v = [load(src, 2, k) for k in range(-1, GROUP + 1)]
        flux = [d[k] * v[k] for k in range(GROUP + 2)]
        for k in range(1, GROUP + 1):
            f = f_ref[row + k - 1]
            d_up, d_down = neighbours(d[k])
            u_up, u_down = neighbours(u[k])
            v_up, v_down = neighbours(v[k])
            t_h = (d_up * u_up - d_down * u_down) + (flux[k + 1] - flux[k - 1])
            t_u = u[k] * (u_up - u_down) + v[k] * ((u[k + 1] - u[k - 1]) - f) + (d_up - d_down)
            t_v = u[k] * ((v_up - v_down) + f) + v[k] * (v[k + 1] - v[k - 1]) + (d[k + 1] - d[k - 1])
            for c, (now, t) in enumerate(((d[k], t_h), (u[k], t_u), (v[k], t_v))):
                new = now - (0.5 * time_step) * t
                if kind == 1:
                    new = 0.75 * load(base, c, k - 1) + 0.25 * new
                elif kind == 2:
                    new = (1.0 / 3.0) * load(base, c, k - 1) + (2.0 / 3.0) * new
                dst[c, pl.ds(pl.multiple_of((row + k - 1) * 8, 8), 8), :] = new
        return carry

    lax.fori_loop(0, -(-rows // GROUP), body, 0)


def half_of(chunk, t_ref):
    swapped = jnp.where(t_ref[2 * LON] == SUB - 1, 1, 0)
    return 1 - swapped if chunk else swapped


def model_kernel(chunk, t_ref, f_ref, s2, s1, s3, s0, out, *bufs):
    x, b, c, y = bufs
    half = half_of(chunk, t_ref)

    def unpack(second):
        for block, s in enumerate((s0, s3, s2, s1)):
            for field in range(3):
                row = ROWS * field
                edge = 3 * ROWS + 2 * HALO * field
                if second:
                    unpack_rows(x, s, field, row + CHUNK - HALO, 1, 0, block)
                    unpack_rows(x, s, field, row + CHUNK - HALO + 1, CHUNK + HALO - 1, 1, block)
                    unpack_rows(x, s, field, edge + HALO, HALO, CHUNK + HALO, block)
                else:
                    unpack_rows(x, s, field, edge, HALO, 0, block)
                    unpack_rows(x, s, field, row, CHUNK + HALO, HALO, block)

    @pl.when(half == 0)
    def _():
        unpack(False)

    @pl.when(half == 1)
    def _():
        unpack(True)

    done = 0
    for _ in range(STEPS):
        for kind, (src, base, dst) in enumerate(((x, x, b), (b, x, c), (c, x, y))):
            done += 1
            stage(src, base, dst, f_ref, done, TILES - 2 * done, kind)
        x, y = y, x
    for field in range(3):
        for r in range(0, CHUNK, 8):
            for s in range(8):
                value = x[field, pl.ds((HALO + r) * 8 + s, 8, stride=8), :]
                out[field, r : r + 8, 128 * s : 128 * s + 128] = (
                    value - 1.0 if field == 0 else value
                )


def model_call(chunk, t, f, pieces):
    return call(
        functools.partial(model_kernel, chunk),
        array(3, CHUNK, NLON),
        [smem_spec()] * 2 + [vmem_spec()] * 4,
        vmem_spec(),
        [pltpu.VMEM((3, (TILES + SPARE) * 8, 128), F32)] * 4,
        10,
    )(t, f, *pieces)


def extra_kernel(t_ref, x, back, e2, e1, e3, e0, buf, sem, sem_out):
    order = ((2, e2), (1, e1), (3, e3), (0, e0))
    at = [aligned(t_ref[j] * ROWS) for j, _ in order]

    def move(src, first):
        pairs = [
            (src.at[:, pl.ds(aligned(row + first), CHUNK), :], buf.at[n])
            for n, row in enumerate(at)
        ]
        for copy in start_all(sem, pairs):
            copy.wait()
        for copy in start_all(sem_out, [(buf.at[n], e) for n, (_, e) in enumerate(order)]):
            copy.wait()

    @pl.when(t_ref[2 * LON] == 0)
    def _():
        move(back, CHUNK)

    @pl.when(t_ref[2 * LON] == SUB - 1)
    def _():
        move(x, 0)


def extra_rows(t, x, back):
    return call(
        extra_kernel,
        [array(3, CHUNK, 256)] * 4,
        [smem_spec(), hbm_spec(), hbm_spec()],
        [hbm_spec()] * 4,
        [pltpu.VMEM((4, 3, CHUNK, 256), F32), dma_sems(4), dma_sems(4)],
        60,
    )(t, x, back)


def rows_kernel(t_ref, x, back, s2, s1, s3, s0, buf, sem, sem_out):
    order = ((2, s2), (1, s1), (3, s3), (0, s0))
    at = [aligned(t_ref[j] * ROWS) for j, _ in order]
    last = t_ref[2 * LON] == SUB - 1

    def move(parts):
        pairs = []
        for n, row in enumerate(at):
            for src, first, count in parts:
                for c in range(3):
                    dst = buf.at[n, pl.ds(ROWS * c + first, count), :]
                    pairs.append((src.at[c, pl.ds(aligned(row + first), count), :], dst))
        copies = start_all(sem, pairs)
        each = 3 * len(parts)
        outs = []
        for n, (_, s) in enumerate(order):
            for copy in copies[each * n : each * n + each]:
                copy.wait()
            buf[n, 3 * ROWS :, :] = jnp.zeros((SENT - 3 * ROWS, 256), F32)
            outs.append(pltpu.make_async_copy(buf.at[n], s, sem_out.at[n]))
            outs[-1].start()
        for copy in outs:
            copy.wait()

    @pl.when(last)
    def _():
        move(((back, 0, CHUNK), (x, CHUNK, CHUNK)))

    @pl.when(jnp.logical_not(last))
    def _():
        move(((x, 0, ROWS),))


def rows_to_send(t, x, back):
    return call(
        rows_kernel,
        [array(SENT, 256)] * 4,
        [smem_spec(), hbm_spec(), hbm_spec()],
        [hbm_spec()] * 4,
        [pltpu.VMEM((4, SENT, 256), F32), dma_sems(24), dma_sems(4)],
        60,
    )(t, x, back)


def edges_kernel(t_ref, x, above, below, *refs):
    outs = refs[4:8]
    edges, ready, sem, sem_out = refs[8:]
    rows = x.shape[1]
    pairs = []
    for q in range(1, LON):
        pairs.append((x.at[:, pl.ds(ROWS * q - 16, 32), :], edges.at[q]))
    pairs += [
        (x.at[:, pl.ds(0, 16), :], edges.at[0, :, pl.ds(16, 16), :]),
        (above, edges.at[0, :, pl.ds(0, 16), :]),
        (x.at[:, pl.ds(rows - 16, 16), :], edges.at[LON, :, pl.ds(0, 16), :]),
        (below, edges.at[LON, :, pl.ds(16, 16), :]),
    ]
    for copy in start_all(sem, pairs):
        copy.wait()
    pairs = []
    for n, j in enumerate((2, 1, 3, 0)):
        for c in range(3):
            edge = 2 * HALO * c
            ready[n, edge : edge + HALO, :] = edges[t_ref[j], c, 16 - HALO : 16, :]
            ready[n, edge + HALO : edge + 2 * HALO, :] = edges[t_ref[j] + 1, c, 16 : 16 + HALO, :]
        ready[n, 6 * HALO :, :] = jnp.zeros((SENT - 3 * ROWS - 6 * HALO, 256), F32)
        pairs.append((ready.at[n], outs[n].at[pl.ds(3 * ROWS, SENT - 3 * ROWS), :]))
    for copy in start_all(sem_out, pairs):
        copy.wait()


def add_edges(t, x, above, below, sent):
    return call(
        edges_kernel,
        [array(SENT, 256)] * 4,
        [smem_spec()] + [hbm_spec()] * 7,
        [hbm_spec()] * 4,
        [
            pltpu.VMEM((LON + 1, 3, 32, 256), F32),
            pltpu.VMEM((4, SENT - 3 * ROWS, 256), F32),
            dma_sems(7),
            dma_sems(4),
        ],
        60,
        input_output_aliases={4: 0, 5: 1, 6: 2, 7: 3},
    )(t, x, above, below, *sent)


def place_first_kernel(t_ref, r2, r1, r3, o0, out, buf, sem, sem_out):
    first = CHUNK * half_of(0, t_ref)
    copies = start_all(sem, [(r, buf.at[j]) for j, r in enumerate((o0, r1, r2, r3))])
    outs = []
    for j, copy in enumerate(copies):
        copy.wait()
        where = out.at[:, pl.ds(aligned(t_ref[LON + j] * ROWS + first), CHUNK), :]
        outs.append(pltpu.make_async_copy(buf.at[j], where, sem_out.at[j]))
        outs[-1].start()
    for copy in outs:
        copy.wait()


def place_first(t, pieces, rows):
    return call(
        place_first_kernel,
        [array(3, rows, 256)],
        [smem_spec()] + [hbm_spec()] * 4,
        [hbm_spec()],
        [pltpu.VMEM((4, 3, CHUNK, 256), F32), dma_sems(4), dma_sems(4)],
        4,
    )(t, *pieces)[0]


def place_second_kernel(t_ref, r2, r1, r3, o0, begun, out, sem):
    first = CHUNK * half_of(1, t_ref)
    pairs = [
        (r, out.at[:, pl.ds(aligned(t_ref[LON + j] * ROWS + first), CHUNK), :])
        for j, r in enumerate((o0, r1, r2, r3))
    ]
    for copy in start_all(sem, pairs):
        copy.wait()


def place_second(t, pieces, begun):
    return call(
        place_second_kernel,
        [array(*begun.shape)],
        [smem_spec()] + [vmem_spec()] * 4 + [hbm_spec()],
        [hbm_spec()],
        [dma_sems(4)],
        4,
        input_output_aliases={5: 0},
    )(t, *pieces, begun)[0]


def cosine_table():
    m = np.arange(NLON // 2 + 1)
    n = np.arange(NLON)
    factor = np.where((m == 0) | (m == NLON // 2), 1.0, 2.0) / NLON
    angle = 2.0 * np.pi / NLON * ((m[:, None] * n[None, :]) % NLON)
    return (factor[:, None] * np.cos(angle)).astype(np.float32)


def split(x):
    high = x.astype(BF16)
    return high, (x - high.astype(F32)).astype(BF16)


def toeplitz(row, size, sign):
    full = pltpu.roll(jnp.broadcast_to(row, (size, size)), 0, 1, stride=1, stride_axis=0)
    if sign < 0:
        c = lax.broadcasted_iota(jnp.int32, (size, size), 0)
        r = lax.broadcasted_iota(jnp.int32, (size, size), 1)
        full = jnp.where(r < c, -full, full)
    return full


def weighting_rows(variances):
    k = jnp.dot(variances, jnp.asarray(cosine_table()), precision=lax.Precision.HIGHEST)
    k0, k1, k2, k3 = (k[:, 256 * j : 256 * j + 256] for j in range(4))
    even = (k0 + k2) * 0.25
    odd = (k1 + k3) * 0.25
    return even + odd, even - odd, (k[:, :512] - k[:, 512:]) * 0.5


def dot3(x, high, low):
    n = x.shape[0]
    xh, xl = split(x)
    y = jnp.dot(jnp.concatenate([xh, xl], axis=0), high, preferred_element_type=F32)
    return y[:n] + y[n:] + jnp.dot(xh, low, preferred_element_type=F32)


def weight_kernel(chunk, t_ref, f_ref, a_ref, b_ref, r_ref, *refs):
    own, other, outs = refs[:4], refs[4:8], refs[8:]
    half = half_of(chunk, t_ref)
    first = t_ref[2 * LON] == 0
    last = t_ref[2 * LON] == SUB - 1
    for c in range(3):
        a = split(toeplitz(a_ref[c : c + 1, :], 256, 1))
        b = split(toeplitz(b_ref[c : c + 1, :], 256, -1))
        r = split(toeplitz(r_ref[c : c + 1, :], 512, -1))
        d = []
        rows = pl.ds(pl.multiple_of(ROWS * c + CHUNK * half, CHUNK), CHUNK)
        for block in range(4):
            f = f_ref[c, :, 256 * block : 256 * block + 256]
            now = own[block][rows, :]
            if chunk == 0:
                prev = jnp.where(first, other[block][rows, :], f)
            else:
                now = jnp.where(last, other[block][c], now)
                prev = jnp.where(first, other[block][c], f)
            d.append(now - prev)
        even, odd = d[0] + d[2], d[1] + d[3]
        x0 = dot3(even + odd, *a)
        y0 = dot3(even - odd, *b)
        w = dot3(jnp.concatenate([d[0] - d[2], d[1] - d[3]], axis=1), *r)
        p, q = x0 + y0, x0 - y0
        outs[0][c] = p + w[:, :256]
        outs[1][c] = q + w[:, 256:]
        outs[2][c] = p - w[:, :256]
        outs[3][c] = q - w[:, 256:]


def weight_call(chunk, t, f, rows, own, other):
    pieces = [*own, *other]
    return call(
        functools.partial(weight_kernel, chunk),
        [array(3, CHUNK, 256)] * 4,
        [smem_spec()] + [vmem_spec()] * 4 + [vmem_spec()] * len(pieces),
        [vmem_spec()] * 4,
        [],
        10,
    )(t, f, *rows, *pieces)


def coriolis_rows(total, first, offsets):
    index = (first + offsets).astype(F32)
    return 2.0 * coriolis_peak * jnp.sin(2.0 * jnp.pi * (index + 0.5) / total)


def ring(count, shift):
    return [(i, (i + shift) % count) for i in range(count)]


def to_next(value, j):
    pairs = [
        (s * LON + a, ((s + 1) % SUB) * LON + (a + j) % LON)
        for s in range(SUB)
        for a in range(LON)
    ]
    return lax.ppermute(value, ("sub", "lon"), pairs)


def to_lon(value, j):
    return lax.ppermute(value, "lon", ring(LON, j))


ORDER = (0, 3, 2, 1)


def shards(segment_launch_values, initial_backdrop, spectral_inverse_variances):
    x = segment_launch_values[0]
    sub, lat, lon = (lax.axis_index(n) for n in ("sub", "lat", "lon"))
    tile_rows = x.shape[1]
    total = tile_rows * lax.axis_size("lat")
    i = jnp.arange(2 * LON + 1, dtype=jnp.int32)
    t = lax.rem(jnp.where(i < LON, lon + i, lon - i + 2 * LON), LON)
    t = jnp.where(i < 2 * LON, t, sub)

    above = lax.ppermute(x[:, tile_rows - 16 :], "lat", ring(8, 1))
    below = lax.ppermute(x[:, :16], "lat", ring(8, -1))
    sent = rows_to_send(t, x, initial_backdrop)
    sent = add_edges(t, x, above, below, sent)
    s2, s1, s3, s0 = (to_next(v, j) for v, j in zip(sent, (2, 1, 3, 0)))
    come = [s0, s3, s2, s1]

    s0, variances, later = lax.optimization_barrier((s0, spectral_inverse_variances, t))
    blocks = extra_rows(later, x, initial_backdrop)
    first_row = lat * tile_rows + lon * ROWS
    offsets = jnp.arange(TILES + SPARE) - HALO
    swapped = jnp.where(sub == SUB - 1, CHUNK, 0)
    f1 = coriolis_rows(total, first_row + swapped, offsets)
    f2 = coriolis_rows(total, first_row - swapped, offsets + CHUNK)
    rows = weighting_rows(variances)
    s3, *tied = lax.optimization_barrier((s3, *rows, *blocks))
    rows, blocks = tied[:3], tied[3:]
    extra = {}
    for j, block in zip((2, 1, 3, 0), blocks):
        pairs = [(s * LON + a, s * LON + (a + j) % LON) for s in (0, SUB - 1) for a in range(LON)]
        extra[j] = lax.ppermute(block, ("sub", "lon"), pairs) if j else block
    extra = [extra[j] for j in (0, 3, 2, 1)]
    own = [sent[3]] + [lax.ppermute(v, "sub", ring(SUB, -1)) for v in (s3, s2, s1)]

    m1 = model_call(0, t, f1, [come[n] for n in (2, 3, 1, 0)])
    o1 = weight_call(0, t, m1, rows, own, come)
    r1 = [to_lon(o1[j], j) if j else o1[j] for j in (2, 1, 3, 0)]
    f2, *tied = lax.optimization_barrier((f2, *o1, *extra))
    o1, extra = tied[:LON], tied[LON:]
    m2 = model_call(1, t, f2, [come[n] for n in (2, 3, 1, 0)])
    o2 = weight_call(1, t, m2, rows, own, extra)
    r2 = [to_lon(o2[j], j) if j else o2[j] for j in (2, 1, 3, 0)]
    return place_second(t, r2, place_first(t, r1, tile_rows))[None]


def solution(mesh):
    return jax.shard_map(
        shards,
        mesh=mesh,
        in_specs=(P("sub", None, "lat", "lon"), P(None, "lat", "lon"), P()),
        out_specs=P("sub", None, "lat", "lon"),
        check_vma=False,
    )
```

```python
import functools

import numpy as np
import jax
import jax.numpy as jnp
from jax import lax
from jax.experimental import pallas as pl
from jax.experimental.pallas import tpu as pltpu
from jax.sharding import PartitionSpec as P

NLON = 1024
STEPS = 3
time_step = 0.5
coriolis_peak = 0.4

SUB = 8
LON = 4
ROWS = 128
HALO = 3 * STEPS
CHUNK = ROWS // 2
SENT = 440
TILES = CHUNK + 2 * HALO
LOOPS = 1
SPARE = 16
F32 = jnp.float32
BF16 = jnp.bfloat16


def vmem_spec():
    return pl.BlockSpec(memory_space=pltpu.VMEM)


def smem_spec():
    return pl.BlockSpec(memory_space=pltpu.SMEM)


def hbm_spec():
    return pl.BlockSpec(memory_space=pltpu.HBM)


def call(kernel, outs, in_specs, out_specs, scratch, mib, **kwargs):
    return pl.pallas_call(
        kernel,
        out_shape=outs,
        in_specs=in_specs,
        out_specs=out_specs,
        scratch_shapes=scratch,
        compiler_params=pltpu.CompilerParams(vmem_limit_bytes=mib << 20),
        cost_estimate=pl.CostEstimate(flops=0, bytes_accessed=1, transcendentals=0),
        **kwargs,
    )


def array(*shape):
    return jax.ShapeDtypeStruct(shape, F32)


def dma_sems(n):
    return pltpu.SemaphoreType.DMA((n,))


def start_all(sem, pairs):
    copies = [pltpu.make_async_copy(a, b, sem.at[n]) for n, (a, b) in enumerate(pairs)]
    for copy in copies:
        copy.start()
    return copies


def aligned(row):
    return pl.multiple_of(row, 16)


def unpack_rows(dst, piece, field, first, count, row0, block):
    done = 0
    while done < count:
        n = min(8, count - done)
        for half in range(2):
            value = piece[first + done : first + done + n, 128 * half : 128 * half + 128]
            start = (row0 + done) * 8 + 2 * block + half
            where = pl.ds(start, n, stride=8) if n > 1 else pl.ds(start, 1)
            dst[field, where, :] = value + 1.0 if field == 0 else value
        done += n


def stage(src, base, dst, f_ref, lo, rows, kind):
    group = rows // LOOPS
    lane = lax.broadcasted_iota(jnp.int32, (8, 128), 1)
    is_first = lane == 0
    is_last = lane == 127

    def neighbours(a):
        up = pltpu.roll(a, 127, 1)
        down = pltpu.roll(a, 1, 1)
        up = jnp.where(is_last, pltpu.roll(up, 7, 0), up)
        down = jnp.where(is_first, pltpu.roll(down, 1, 0), down)
        return up, down

    def body(g, carry):
        row = lo + g * group

        def load(ref, c, k):
            return ref[c, pl.ds(pl.multiple_of((row + k) * 8, 8), 8), :]

        d = [load(src, 0, k) for k in range(-1, group + 1)]
        u = [load(src, 1, k) for k in range(-1, group + 1)]
        v = [load(src, 2, k) for k in range(-1, group + 1)]
        flux = [d[k] * v[k] for k in range(group + 2)]
        for k in range(1, group + 1):
            f = f_ref[row + k - 1]
            d_up, d_down = neighbours(d[k])
            u_up, u_down = neighbours(u[k])
            v_up, v_down = neighbours(v[k])
            t_h = (d_up * u_up - d_down * u_down) + (flux[k + 1] - flux[k - 1])
            t_u = u[k] * (u_up - u_down) + v[k] * ((u[k + 1] - u[k - 1]) - f) + (d_up - d_down)
            t_v = u[k] * ((v_up - v_down) + f) + v[k] * (v[k + 1] - v[k - 1]) + (d[k + 1] - d[k - 1])
            for c, (now, t) in enumerate(((d[k], t_h), (u[k], t_u), (v[k], t_v))):
                new = now - (0.5 * time_step) * t
                if kind == 1:
                    new = 0.75 * load(base, c, k - 1) + 0.25 * new
                elif kind == 2:
                    new = (1.0 / 3.0) * load(base, c, k - 1) + (2.0 / 3.0) * new
                dst[c, pl.ds(pl.multiple_of((row + k - 1) * 8, 8), 8), :] = new
        return carry

    lax.fori_loop(0, LOOPS, body, 0)


def half_of(chunk, t_ref):
    swapped = jnp.where(t_ref[2 * LON] == SUB - 1, 1, 0)
    return 1 - swapped if chunk else swapped


def model_kernel(chunk, t_ref, f_ref, s0, s3, s2, s1, out, *bufs):
    x, b, c, y = bufs
    half = half_of(chunk, t_ref)

    def unpack(second):
        for block, s in enumerate((s0, s3, s2, s1)):
            for field in range(3):
                row = ROWS * field
                edge = 3 * ROWS + 2 * HALO * field
                if second:
                    unpack_rows(x, s, field, row + CHUNK - HALO, 1, 0, block)
                    unpack_rows(x, s, field, row + CHUNK - HALO + 1, CHUNK + HALO - 1, 1, block)
                    unpack_rows(x, s, field, edge + HALO, HALO, CHUNK + HALO, block)
                else:
                    unpack_rows(x, s, field, edge, HALO, 0, block)
                    unpack_rows(x, s, field, row, CHUNK + HALO, HALO, block)

    @pl.when(half == 0)
    def _():
        unpack(False)

    @pl.when(half == 1)
    def _():
        unpack(True)

    done = 0
    for _ in range(STEPS):
        for kind, (src, base, dst) in enumerate(((x, x, b), (b, x, c), (c, x, y))):
            done += 1
            stage(src, base, dst, f_ref, done, TILES - 2 * done, kind)
        x, y = y, x
    for field in range(3):
        for r in range(0, CHUNK, 8):
            for s in range(8):
                value = x[field, pl.ds((HALO + r) * 8 + s, 8, stride=8), :]
                out[field, r : r + 8, 128 * s : 128 * s + 128] = (
                    value - 1.0 if field == 0 else value
                )


def model_call(chunk, t, f, pieces):
    return call(
        functools.partial(model_kernel, chunk),
        array(3, CHUNK, NLON),
        [smem_spec()] * 2 + [vmem_spec()] * 4,
        vmem_spec(),
        [pltpu.VMEM((3, (TILES + SPARE) * 8, 128), F32)] * 4,
        10,
    )(t, f, *pieces)


def extra_kernel(t_ref, x, back, e2, e1, e3, e0, buf, sem, sem_out):
    order = ((2, e2), (1, e1), (3, e3), (0, e0))
    at = [aligned(t_ref[j] * ROWS) for j, _ in order]

    def move(src, first):
        pairs = [
            (src.at[:, pl.ds(aligned(row + first), CHUNK), :], buf.at[n])
            for n, row in enumerate(at)
        ]
        for copy in start_all(sem, pairs):
            copy.wait()
        for copy in start_all(sem_out, [(buf.at[n], e) for n, (_, e) in enumerate(order)]):
            copy.wait()

    @pl.when(t_ref[2 * LON] == 0)
    def _():
        move(back, CHUNK)

    @pl.when(t_ref[2 * LON] == SUB - 1)
    def _():
        move(x, 0)


def extra_rows(t, x, back):
    return call(
        extra_kernel,
        [array(3, CHUNK, 256)] * 4,
        [smem_spec(), hbm_spec(), hbm_spec()],
        [hbm_spec()] * 4,
        [pltpu.VMEM((4, 3, CHUNK, 256), F32), dma_sems(4), dma_sems(4)],
        60,
    )(t, x, back)


def rows_kernel(t_ref, x, back, s2, s1, s3, s0, buf, sem, sem_out):
    order = ((2, s2), (1, s1), (3, s3), (0, s0))
    at = [aligned(t_ref[j] * ROWS) for j, _ in order]
    last = t_ref[2 * LON] == SUB - 1

    def move(parts):
        pairs = []
        for n, row in enumerate(at):
            for src, first, count in parts:
                for c in range(3):
                    dst = buf.at[n, pl.ds(ROWS * c + first, count), :]
                    pairs.append((src.at[c, pl.ds(aligned(row + first), count), :], dst))
        copies = start_all(sem, pairs)
        each = 3 * len(parts)
        outs = []
        for n, (_, s) in enumerate(order):
            for copy in copies[each * n : each * n + each]:
                copy.wait()
            buf[n, 3 * ROWS :, :] = jnp.zeros((SENT - 3 * ROWS, 256), F32)
            outs.append(pltpu.make_async_copy(buf.at[n], s, sem_out.at[n]))
            outs[-1].start()
        for copy in outs:
            copy.wait()

    @pl.when(last)
    def _():
        move(((back, 0, CHUNK), (x, CHUNK, CHUNK)))

    @pl.when(jnp.logical_not(last))
    def _():
        move(((x, 0, ROWS),))


def rows_to_send(t, x, back):
    return call(
        rows_kernel,
        [array(SENT, 256)] * 4,
        [smem_spec(), hbm_spec(), hbm_spec()],
        [hbm_spec()] * 4,
        [pltpu.VMEM((4, SENT, 256), F32), dma_sems(24), dma_sems(4)],
        60,
    )(t, x, back)


def edges_kernel(t_ref, x, above, below, *refs):
    outs = refs[4:8]
    edges, ready, sem, sem_out = refs[8:]
    rows = x.shape[1]
    pairs = []
    for q in range(1, LON):
        pairs.append((x.at[:, pl.ds(ROWS * q - 16, 32), :], edges.at[q]))
    pairs += [
        (x.at[:, pl.ds(0, 16), :], edges.at[0, :, pl.ds(16, 16), :]),
        (above, edges.at[0, :, pl.ds(0, 16), :]),
        (x.at[:, pl.ds(rows - 16, 16), :], edges.at[LON, :, pl.ds(0, 16), :]),
        (below, edges.at[LON, :, pl.ds(16, 16), :]),
    ]
    for copy in start_all(sem, pairs):
        copy.wait()
    pairs = []
    for n, j in enumerate((2, 1, 3, 0)):
        for c in range(3):
            edge = 2 * HALO * c
            ready[n, edge : edge + HALO, :] = edges[t_ref[j], c, 16 - HALO : 16, :]
            ready[n, edge + HALO : edge + 2 * HALO, :] = edges[t_ref[j] + 1, c, 16 : 16 + HALO, :]
        ready[n, 6 * HALO :, :] = jnp.zeros((SENT - 3 * ROWS - 6 * HALO, 256), F32)
        pairs.append((ready.at[n], outs[n].at[pl.ds(3 * ROWS, SENT - 3 * ROWS), :]))
    for copy in start_all(sem_out, pairs):
        copy.wait()


def add_edges(t, x, above, below, sent):
    return call(
        edges_kernel,
        [array(SENT, 256)] * 4,
        [smem_spec()] + [hbm_spec()] * 7,
        [hbm_spec()] * 4,
        [
            pltpu.VMEM((LON + 1, 3, 32, 256), F32),
            pltpu.VMEM((4, SENT - 3 * ROWS, 256), F32),
            dma_sems(7),
            dma_sems(4),
        ],
        60,
        input_output_aliases={4: 0, 5: 1, 6: 2, 7: 3},
    )(t, x, above, below, *sent)


def place_first_kernel(t_ref, o0, r1, r2, r3, out, buf, sem, sem_out):
    first = CHUNK * half_of(0, t_ref)
    copies = start_all(sem, [(r, buf.at[j]) for j, r in enumerate((o0, r1, r2, r3))])
    outs = []
    for j, copy in enumerate(copies):
        copy.wait()
        where = out.at[:, pl.ds(aligned(t_ref[LON + j] * ROWS + first), CHUNK), :]
        outs.append(pltpu.make_async_copy(buf.at[j], where, sem_out.at[j]))
        outs[-1].start()
    for copy in outs:
        copy.wait()


def place_first(t, pieces, rows):
    return call(
        place_first_kernel,
        [array(3, rows, 256)],
        [smem_spec()] + [hbm_spec()] * 4,
        [hbm_spec()],
        [pltpu.VMEM((4, 3, CHUNK, 256), F32), dma_sems(4), dma_sems(4)],
        4,
    )(t, *pieces)[0]


def place_second_kernel(t_ref, o0, r1, r2, r3, begun, out, sem):
    first = CHUNK * half_of(1, t_ref)
    pairs = [
        (r, out.at[:, pl.ds(aligned(t_ref[LON + j] * ROWS + first), CHUNK), :])
        for j, r in enumerate((o0, r1, r2, r3))
    ]
    for copy in start_all(sem, pairs):
        copy.wait()


def place_second(t, pieces, begun):
    return call(
        place_second_kernel,
        [array(*begun.shape)],
        [smem_spec()] + [vmem_spec()] * 4 + [hbm_spec()],
        [hbm_spec()],
        [dma_sems(4)],
        4,
        input_output_aliases={5: 0},
    )(t, *pieces, begun)[0]


def cosine_table():
    m = np.arange(NLON // 2 + 1)
    n = np.arange(NLON)
    factor = np.where((m == 0) | (m == NLON // 2), 1.0, 2.0) / NLON
    angle = 2.0 * np.pi / NLON * ((m[:, None] * n[None, :]) % NLON)
    return (factor[:, None] * np.cos(angle)).astype(np.float32)


def split(x):
    high = x.astype(BF16)
    return high, (x - high.astype(F32)).astype(BF16)


def toeplitz(row, size, sign):
    full = pltpu.roll(jnp.broadcast_to(row, (size, size)), 0, 1, stride=1, stride_axis=0)
    if sign < 0:
        c = lax.broadcasted_iota(jnp.int32, (size, size), 0)
        r = lax.broadcasted_iota(jnp.int32, (size, size), 1)
        full = jnp.where(r < c, -full, full)
    return full


def weighting_rows(variances):
    k = jnp.dot(variances, jnp.asarray(cosine_table()), precision=lax.Precision.HIGHEST)
    k0, k1, k2, k3 = (k[:, 256 * j : 256 * j + 256] for j in range(4))
    even = (k0 + k2) * 0.25
    odd = (k1 + k3) * 0.25
    return even + odd, even - odd, (k[:, :512] - k[:, 512:]) * 0.5


def dot3(x, high, low):
    n = x.shape[0]
    xh, xl = split(x)
    y = jnp.dot(jnp.concatenate([xh, xl], axis=0), high, preferred_element_type=F32)
    return y[:n] + y[n:] + jnp.dot(xh, low, preferred_element_type=F32)


def weight_kernel(chunk, t_ref, f_ref, a_ref, b_ref, r_ref, *refs):
    own, other, outs = refs[:4], refs[4:8], refs[8:]
    half = half_of(chunk, t_ref)
    first = t_ref[2 * LON] == 0
    last = t_ref[2 * LON] == SUB - 1
    for c in range(3):
        a = split(toeplitz(a_ref[c : c + 1, :], 256, 1))
        b = split(toeplitz(b_ref[c : c + 1, :], 256, -1))
        r = split(toeplitz(r_ref[c : c + 1, :], 512, -1))
        d = []
        rows = pl.ds(pl.multiple_of(ROWS * c + CHUNK * half, CHUNK), CHUNK)
        for block in range(4):
            f = f_ref[c, :, 256 * block : 256 * block + 256]
            now = own[block][rows, :]
            if chunk == 0:
                prev = jnp.where(first, other[block][rows, :], f)
            else:
                now = jnp.where(last, other[block][c], now)
                prev = jnp.where(first, other[block][c], f)
            d.append(now - prev)
        even, odd = d[0] + d[2], d[1] + d[3]
        x0 = dot3(even + odd, *a)
        y0 = dot3(even - odd, *b)
        w = dot3(jnp.concatenate([d[0] - d[2], d[1] - d[3]], axis=1), *r)
        p, q = x0 + y0, x0 - y0
        outs[0][c] = p + w[:, :256]
        outs[1][c] = q + w[:, 256:]
        outs[2][c] = p - w[:, :256]
        outs[3][c] = q - w[:, 256:]


def weight_call(chunk, t, f, rows, own, other):
    pieces = [*own, *other]
    return call(
        functools.partial(weight_kernel, chunk),
        [array(3, CHUNK, 256)] * 4,
        [smem_spec()] + [vmem_spec()] * 4 + [vmem_spec()] * len(pieces),
        [vmem_spec()] * 4,
        [],
        10,
    )(t, f, *rows, *pieces)


def coriolis_rows(total, first, offsets):
    index = (first + offsets).astype(F32)
    return 2.0 * coriolis_peak * jnp.sin(2.0 * jnp.pi * (index + 0.5) / total)


def ring(count, shift):
    return [(i, (i + shift) % count) for i in range(count)]


def to_next(value, j):
    pairs = [
        (s * LON + a, ((s + 1) % SUB) * LON + (a + j) % LON)
        for s in range(SUB)
        for a in range(LON)
    ]
    return lax.ppermute(value, ("sub", "lon"), pairs)


def to_lon(value, j):
    return lax.ppermute(value, "lon", ring(LON, j))


ORDER = (0, 3, 2, 1)


def shards(segment_launch_values, initial_backdrop, spectral_inverse_variances):
    x = segment_launch_values[0]
    sub, lat, lon = (lax.axis_index(n) for n in ("sub", "lat", "lon"))
    tile_rows = x.shape[1]
    total = tile_rows * lax.axis_size("lat")
    i = jnp.arange(2 * LON + 1, dtype=jnp.int32)
    t = lax.rem(jnp.where(i < LON, lon + i, lon - i + 2 * LON), LON)
    t = jnp.where(i < 2 * LON, t, sub)

    above = lax.ppermute(x[:, tile_rows - 16 :], "lat", ring(8, 1))
    below = lax.ppermute(x[:, :16], "lat", ring(8, -1))
    sent = rows_to_send(t, x, initial_backdrop)
    sent = add_edges(t, x, above, below, sent)
    s2, s1, s3, s0 = (to_next(v, j) for v, j in zip(sent, (2, 1, 3, 0)))
    come = [s0, s3, s2, s1]

    s0, variances, later = lax.optimization_barrier((s0, spectral_inverse_variances, t))
    blocks = extra_rows(later, x, initial_backdrop)
    first_row = lat * tile_rows + lon * ROWS
    offsets = jnp.arange(TILES + SPARE) - HALO
    swapped = jnp.where(sub == SUB - 1, CHUNK, 0)
    f1 = coriolis_rows(total, first_row + swapped, offsets)
    f2 = coriolis_rows(total, first_row - swapped, offsets + CHUNK)
    rows = weighting_rows(variances)
    s3, *tied = lax.optimization_barrier((s3, *rows, *blocks))
    rows, blocks = tied[:3], tied[3:]
    extra = {}
    for j, block in zip((2, 1, 3, 0), blocks):
        pairs = [(s * LON + a, s * LON + (a + j) % LON) for s in (0, SUB - 1) for a in range(LON)]
        extra[j] = lax.ppermute(block, ("sub", "lon"), pairs) if j else block
    extra = [extra[j] for j in (0, 3, 2, 1)]
    own = [sent[3]] + [lax.ppermute(v, "sub", ring(SUB, -1)) for v in (s3, s2, s1)]

    m1 = model_call(0, t, f1, come)
    o1 = weight_call(0, t, m1, rows, own, come)
    r1 = [to_lon(o1[j], j) if j else o1[j] for j in range(LON)]
    f2, *tied = lax.optimization_barrier((f2, *o1, *extra))
    o1, extra = tied[:LON], tied[LON:]
    m2 = model_call(1, t, f2, come)
    o2 = weight_call(1, t, m2, rows, own, extra)
    r2 = [to_lon(o2[j], j) if j else o2[j] for j in range(LON)]
    return place_second(t, r2, place_first(t, r1, tile_rows))[None]


def solution(mesh):
    return jax.shard_map(
        shards,
        mesh=mesh,
        in_specs=(P("sub", None, "lat", "lon"), P(None, "lat", "lon"), P()),
        out_specs=P("sub", None, "lat", "lon"),
        check_vma=False,
    )
```

```python
import functools

import numpy as np
import jax
import jax.numpy as jnp
from jax import lax
from jax.experimental import pallas as pl
from jax.experimental.pallas import tpu as pltpu
from jax.sharding import PartitionSpec as P

NLON = 1024
STEPS = 3
time_step = 0.5
coriolis_peak = 0.4

SUB = 8
LON = 4
ROWS = 128
HALO = 3 * STEPS
CHUNK = ROWS // 2
SENT = 440
TILES = CHUNK + 2 * HALO
LOOPS = 1
SPARE = 16
F32 = jnp.float32
BF16 = jnp.bfloat16


def vmem_spec():
    return pl.BlockSpec(memory_space=pltpu.VMEM)


def smem_spec():
    return pl.BlockSpec(memory_space=pltpu.SMEM)


def hbm_spec():
    return pl.BlockSpec(memory_space=pltpu.HBM)


def call(kernel, outs, in_specs, out_specs, scratch, mib, **kwargs):
    return pl.pallas_call(
        kernel,
        out_shape=outs,
        in_specs=in_specs,
        out_specs=out_specs,
        scratch_shapes=scratch,
        compiler_params=pltpu.CompilerParams(vmem_limit_bytes=mib << 20),
        cost_estimate=pl.CostEstimate(flops=0, bytes_accessed=1, transcendentals=0),
        **kwargs,
    )


def array(*shape):
    return jax.ShapeDtypeStruct(shape, F32)


def dma_sems(n):
    return pltpu.SemaphoreType.DMA((n,))


def start_all(sem, pairs):
    copies = [pltpu.make_async_copy(a, b, sem.at[n]) for n, (a, b) in enumerate(pairs)]
    for copy in copies:
        copy.start()
    return copies


def aligned(row):
    return pl.multiple_of(row, 16)


def unpack_rows(dst, piece, field, first, count, row0, block):
    done = 0
    while done < count:
        n = min(8, count - done)
        for half in range(2):
            value = piece[first + done : first + done + n, 128 * half : 128 * half + 128]
            start = (row0 + done) * 8 + 2 * block + half
            where = pl.ds(start, n, stride=8) if n > 1 else pl.ds(start, 1)
            dst[field, where, :] = value + 1.0 if field == 0 else value
        done += n


def stage(src, base, dst, f_ref, lo, rows, kind):
    group = rows // LOOPS
    lane = lax.broadcasted_iota(jnp.int32, (8, 128), 1)
    is_first = lane == 0
    is_last = lane == 127

    def neighbours(a):
        up = pltpu.roll(a, 127, 1)
        down = pltpu.roll(a, 1, 1)
        up = jnp.where(is_last, pltpu.roll(up, 7, 0), up)
        down = jnp.where(is_first, pltpu.roll(down, 1, 0), down)
        return up, down

    def body(g, carry):
        row = lo + g * group

        def load(ref, c, k):
            return ref[c, pl.ds(pl.multiple_of((row + k) * 8, 8), 8), :]

        d = [load(src, 0, k) for k in range(-1, group + 1)]
        u = [load(src, 1, k) for k in range(-1, group + 1)]
        v = [load(src, 2, k) for k in range(-1, group + 1)]
        flux = [d[k] * v[k] for k in range(group + 2)]
        for k in range(1, group + 1):
            f = f_ref[row + k - 1]
            d_up, d_down = neighbours(d[k])
            u_up, u_down = neighbours(u[k])
            v_up, v_down = neighbours(v[k])
            t_h = (d_up * u_up - d_down * u_down) + (flux[k + 1] - flux[k - 1])
            t_u = u[k] * (u_up - u_down) + v[k] * ((u[k + 1] - u[k - 1]) - f) + (d_up - d_down)
            t_v = u[k] * ((v_up - v_down) + f) + v[k] * (v[k + 1] - v[k - 1]) + (d[k + 1] - d[k - 1])
            for c, (now, t) in enumerate(((d[k], t_h), (u[k], t_u), (v[k], t_v))):
                new = now - (0.5 * time_step) * t
                if kind == 1:
                    new = 0.75 * load(base, c, k - 1) + 0.25 * new
                elif kind == 2:
                    new = (1.0 / 3.0) * load(base, c, k - 1) + (2.0 / 3.0) * new
                dst[c, pl.ds(pl.multiple_of((row + k - 1) * 8, 8), 8), :] = new
        return carry

    lax.fori_loop(0, LOOPS, body, 0)


def half_of(chunk, t_ref):
    swapped = jnp.where(t_ref[2 * LON] == SUB - 1, 1, 0)
    return 1 - swapped if chunk else swapped


def model_kernel(chunk, t_ref, f_ref, s0, s3, s2, s1, out, *bufs):
    x, b, c, y = bufs
    half = half_of(chunk, t_ref)

    def unpack(second):
        for block, s in enumerate((s0, s3, s2, s1)):
            for field in range(3):
                row = ROWS * field
                edge = 3 * ROWS + 2 * HALO * field
                if second:
                    unpack_rows(x, s, field, row + CHUNK - HALO, 1, 0, block)
                    unpack_rows(x, s, field, row + CHUNK - HALO + 1, CHUNK + HALO - 1, 1, block)
                    unpack_rows(x, s, field, edge + HALO, HALO, CHUNK + HALO, block)
                else:
                    unpack_rows(x, s, field, edge, HALO, 0, block)
                    unpack_rows(x, s, field, row, CHUNK + HALO, HALO, block)

    @pl.when(half == 0)
    def _():
        unpack(False)

    @pl.when(half == 1)
    def _():
        unpack(True)

    done = 0
    for _ in range(STEPS):
        for kind, (src, base, dst) in enumerate(((x, x, b), (b, x, c), (c, x, y))):
            done += 1
            stage(src, base, dst, f_ref, done, TILES - 2 * done, kind)
        x, y = y, x
    for field in range(3):
        for r in range(0, CHUNK, 8):
            for s in range(8):
                value = x[field, pl.ds((HALO + r) * 8 + s, 8, stride=8), :]
                out[field, r : r + 8, 128 * s : 128 * s + 128] = (
                    value - 1.0 if field == 0 else value
                )


def model_call(chunk, t, f, pieces):
    return call(
        functools.partial(model_kernel, chunk),
        array(3, CHUNK, NLON),
        [smem_spec()] * 2 + [vmem_spec()] * 4,
        vmem_spec(),
        [pltpu.VMEM((3, (TILES + SPARE) * 8, 128), F32)] * 4,
        10,
    )(t, f, *pieces)


def extra_kernel(t_ref, x, back, e2, e1, e3, e0, buf, sem, sem_out):
    order = ((2, e2), (1, e1), (3, e3), (0, e0))
    at = [aligned(t_ref[j] * ROWS) for j, _ in order]

    def move(src, first):
        pairs = [
            (src.at[:, pl.ds(aligned(row + first), CHUNK), :], buf.at[n])
            for n, row in enumerate(at)
        ]
        for copy in start_all(sem, pairs):
            copy.wait()
        for copy in start_all(sem_out, [(buf.at[n], e) for n, (_, e) in enumerate(order)]):
            copy.wait()

    @pl.when(t_ref[2 * LON] == 0)
    def _():
        move(back, CHUNK)

    @pl.when(t_ref[2 * LON] == SUB - 1)
    def _():
        move(x, 0)


def extra_rows(t, x, back):
    return call(
        extra_kernel,
        [array(3, CHUNK, 256)] * 4,
        [smem_spec(), hbm_spec(), hbm_spec()],
        [hbm_spec()] * 4,
        [pltpu.VMEM((4, 3, CHUNK, 256), F32), dma_sems(4), dma_sems(4)],
        60,
    )(t, x, back)


def rows_kernel(t_ref, x, back, s2, s1, s3, s0, buf, sem, sem_out):
    order = ((2, s2), (1, s1), (3, s3), (0, s0))
    at = [aligned(t_ref[j] * ROWS) for j, _ in order]
    last = t_ref[2 * LON] == SUB - 1

    def move(parts):
        pairs = []
        for n, row in enumerate(at):
            for src, first, count in parts:
                for c in range(3):
                    dst = buf.at[n, pl.ds(ROWS * c + first, count), :]
                    pairs.append((src.at[c, pl.ds(aligned(row + first), count), :], dst))
        copies = start_all(sem, pairs)
        each = 3 * len(parts)
        outs = []
        for n, (_, s) in enumerate(order):
            for copy in copies[each * n : each * n + each]:
                copy.wait()
            buf[n, 3 * ROWS :, :] = jnp.zeros((SENT - 3 * ROWS, 256), F32)
            outs.append(pltpu.make_async_copy(buf.at[n], s, sem_out.at[n]))
            outs[-1].start()
        for copy in outs:
            copy.wait()

    @pl.when(last)
    def _():
        move(((back, 0, CHUNK), (x, CHUNK, CHUNK)))

    @pl.when(jnp.logical_not(last))
    def _():
        move(((x, 0, ROWS),))


def rows_to_send(t, x, back):
    return call(
        rows_kernel,
        [array(SENT, 256)] * 4,
        [smem_spec(), hbm_spec(), hbm_spec()],
        [hbm_spec()] * 4,
        [pltpu.VMEM((4, SENT, 256), F32), dma_sems(24), dma_sems(4)],
        60,
    )(t, x, back)


def edges_kernel(t_ref, x, above, below, *refs):
    outs = refs[4:8]
    edges, ready, sem, sem_out = refs[8:]
    rows = x.shape[1]
    pairs = []
    for q in range(1, LON):
        pairs.append((x.at[:, pl.ds(ROWS * q - 16, 32), :], edges.at[q]))
    pairs += [
        (x.at[:, pl.ds(0, 16), :], edges.at[0, :, pl.ds(16, 16), :]),
        (above, edges.at[0, :, pl.ds(0, 16), :]),
        (x.at[:, pl.ds(rows - 16, 16), :], edges.at[LON, :, pl.ds(0, 16), :]),
        (below, edges.at[LON, :, pl.ds(16, 16), :]),
    ]
    for copy in start_all(sem, pairs):
        copy.wait()
    pairs = []
    for n, j in enumerate((2, 1, 3, 0)):
        for c in range(3):
            edge = 2 * HALO * c
            ready[n, edge : edge + HALO, :] = edges[t_ref[j], c, 16 - HALO : 16, :]
            ready[n, edge + HALO : edge + 2 * HALO, :] = edges[t_ref[j] + 1, c, 16 : 16 + HALO, :]
        ready[n, 6 * HALO :, :] = jnp.zeros((SENT - 3 * ROWS - 6 * HALO, 256), F32)
        pairs.append((ready.at[n], outs[n].at[pl.ds(3 * ROWS, SENT - 3 * ROWS), :]))
    for copy in start_all(sem_out, pairs):
        copy.wait()


def add_edges(t, x, above, below, sent):
    return call(
        edges_kernel,
        [array(SENT, 256)] * 4,
        [smem_spec()] + [hbm_spec()] * 7,
        [hbm_spec()] * 4,
        [
            pltpu.VMEM((LON + 1, 3, 32, 256), F32),
            pltpu.VMEM((4, SENT - 3 * ROWS, 256), F32),
            dma_sems(7),
            dma_sems(4),
        ],
        60,
        input_output_aliases={4: 0, 5: 1, 6: 2, 7: 3},
    )(t, x, above, below, *sent)


def place_first_kernel(t_ref, r2, r1, r3, o0, out, buf, sem, sem_out):
    first = CHUNK * half_of(0, t_ref)
    copies = start_all(sem, [(r, buf.at[j]) for j, r in enumerate((o0, r1, r2, r3))])
    outs = []
    for j, copy in enumerate(copies):
        copy.wait()
        where = out.at[:, pl.ds(aligned(t_ref[LON + j] * ROWS + first), CHUNK), :]
        outs.append(pltpu.make_async_copy(buf.at[j], where, sem_out.at[j]))
        outs[-1].start()
    for copy in outs:
        copy.wait()


def place_first(t, pieces, rows):
    return call(
        place_first_kernel,
        [array(3, rows, 256)],
        [smem_spec()] + [hbm_spec()] * 4,
        [hbm_spec()],
        [pltpu.VMEM((4, 3, CHUNK, 256), F32), dma_sems(4), dma_sems(4)],
        4,
    )(t, *pieces)[0]


def place_second_kernel(t_ref, r2, r1, r3, o0, begun, out, sem):
    first = CHUNK * half_of(1, t_ref)
    pairs = [
        (r, out.at[:, pl.ds(aligned(t_ref[LON + j] * ROWS + first), CHUNK), :])
        for j, r in enumerate((o0, r1, r2, r3))
    ]
    for copy in start_all(sem, pairs):
        copy.wait()


def place_second(t, pieces, begun):
    return call(
        place_second_kernel,
        [array(*begun.shape)],
        [smem_spec()] + [vmem_spec()] * 4 + [hbm_spec()],
        [hbm_spec()],
        [dma_sems(4)],
        4,
        input_output_aliases={5: 0},
    )(t, *pieces, begun)[0]


def cosine_table():
    m = np.arange(NLON // 2 + 1)
    n = np.arange(NLON)
    factor = np.where((m == 0) | (m == NLON // 2), 1.0, 2.0) / NLON
    angle = 2.0 * np.pi / NLON * ((m[:, None] * n[None, :]) % NLON)
    return (factor[:, None] * np.cos(angle)).astype(np.float32)


def split(x):
    high = x.astype(BF16)
    return high, (x - high.astype(F32)).astype(BF16)


def toeplitz(row, size, sign):
    full = pltpu.roll(jnp.broadcast_to(row, (size, size)), 0, 1, stride=1, stride_axis=0)
    if sign < 0:
        c = lax.broadcasted_iota(jnp.int32, (size, size), 0)
        r = lax.broadcasted_iota(jnp.int32, (size, size), 1)
        full = jnp.where(r < c, -full, full)
    return full


def weighting_rows(variances):
    k = jnp.dot(variances, jnp.asarray(cosine_table()), precision=lax.Precision.HIGHEST)
    k0, k1, k2, k3 = (k[:, 256 * j : 256 * j + 256] for j in range(4))
    even = (k0 + k2) * 0.25
    odd = (k1 + k3) * 0.25
    return even + odd, even - odd, (k[:, :512] - k[:, 512:]) * 0.5


def dot3(x, high, low):
    n = x.shape[0]
    xh, xl = split(x)
    y = jnp.dot(jnp.concatenate([xh, xl], axis=0), high, preferred_element_type=F32)
    return y[:n] + y[n:] + jnp.dot(xh, low, preferred_element_type=F32)


def weight_kernel(chunk, t_ref, f_ref, a_ref, b_ref, r_ref, *refs):
    own, other, outs = refs[:4], refs[4:8], refs[8:]
    half = half_of(chunk, t_ref)
    first = t_ref[2 * LON] == 0
    last = t_ref[2 * LON] == SUB - 1
    for c in range(3):
        a = split(toeplitz(a_ref[c : c + 1, :], 256, 1))
        b = split(toeplitz(b_ref[c : c + 1, :], 256, -1))
        r = split(toeplitz(r_ref[c : c + 1, :], 512, -1))
        d = []
        rows = pl.ds(pl.multiple_of(ROWS * c + CHUNK * half, CHUNK), CHUNK)
        for block in range(4):
            f = f_ref[c, :, 256 * block : 256 * block + 256]
            now = own[block][rows, :]
            if chunk == 0:
                prev = jnp.where(first, other[block][rows, :], f)
            else:
                now = jnp.where(last, other[block][c], now)
                prev = jnp.where(first, other[block][c], f)
            d.append(now - prev)
        even, odd = d[0] + d[2], d[1] + d[3]
        x0 = dot3(even + odd, *a)
        y0 = dot3(even - odd, *b)
        w = dot3(jnp.concatenate([d[0] - d[2], d[1] - d[3]], axis=1), *r)
        p, q = x0 + y0, x0 - y0
        outs[0][c] = p + w[:, :256]
        outs[1][c] = q + w[:, 256:]
        outs[2][c] = p - w[:, :256]
        outs[3][c] = q - w[:, 256:]


def weight_call(chunk, t, f, rows, own, other):
    pieces = [*own, *other]
    return call(
        functools.partial(weight_kernel, chunk),
        [array(3, CHUNK, 256)] * 4,
        [smem_spec()] + [vmem_spec()] * 4 + [vmem_spec()] * len(pieces),
        [vmem_spec()] * 4,
        [],
        10,
    )(t, f, *rows, *pieces)


def coriolis_rows(total, first, offsets):
    index = (first + offsets).astype(F32)
    return 2.0 * coriolis_peak * jnp.sin(2.0 * jnp.pi * (index + 0.5) / total)


def ring(count, shift):
    return [(i, (i + shift) % count) for i in range(count)]


def to_next(value, j):
    pairs = [
        (s * LON + a, ((s + 1) % SUB) * LON + (a + j) % LON)
        for s in range(SUB)
        for a in range(LON)
    ]
    return lax.ppermute(value, ("sub", "lon"), pairs)


def to_lon(value, j):
    return lax.ppermute(value, "lon", ring(LON, j))


ORDER = (0, 3, 2, 1)


def shards(segment_launch_values, initial_backdrop, spectral_inverse_variances):
    x = segment_launch_values[0]
    sub, lat, lon = (lax.axis_index(n) for n in ("sub", "lat", "lon"))
    tile_rows = x.shape[1]
    total = tile_rows * lax.axis_size("lat")
    i = jnp.arange(2 * LON + 1, dtype=jnp.int32)
    t = lax.rem(jnp.where(i < LON, lon + i, lon - i + 2 * LON), LON)
    t = jnp.where(i < 2 * LON, t, sub)

    above = lax.ppermute(x[:, tile_rows - 16 :], "lat", ring(8, 1))
    below = lax.ppermute(x[:, :16], "lat", ring(8, -1))
    sent = rows_to_send(t, x, initial_backdrop)
    sent = add_edges(t, x, above, below, sent)
    s2, s1, s3, s0 = (to_next(v, j) for v, j in zip(sent, (2, 1, 3, 0)))
    come = [s0, s3, s2, s1]

    s0, variances, later = lax.optimization_barrier((s0, spectral_inverse_variances, t))
    blocks = extra_rows(later, x, initial_backdrop)
    first_row = lat * tile_rows + lon * ROWS
    offsets = jnp.arange(TILES + SPARE) - HALO
    swapped = jnp.where(sub == SUB - 1, CHUNK, 0)
    f1 = coriolis_rows(total, first_row + swapped, offsets)
    f2 = coriolis_rows(total, first_row - swapped, offsets + CHUNK)
    rows = weighting_rows(variances)
    s3, *tied = lax.optimization_barrier((s3, *rows, *blocks))
    rows, blocks = tied[:3], tied[3:]
    extra = {}
    for j, block in zip((2, 1, 3, 0), blocks):
        pairs = [(s * LON + a, s * LON + (a + j) % LON) for s in (0, SUB - 1) for a in range(LON)]
        extra[j] = lax.ppermute(block, ("sub", "lon"), pairs) if j else block
    extra = [extra[j] for j in (0, 3, 2, 1)]
    own = [sent[3]] + [lax.ppermute(v, "sub", ring(SUB, -1)) for v in (s3, s2, s1)]

    m1 = model_call(0, t, f1, come)
    o1 = weight_call(0, t, m1, rows, own, come)
    r1 = [to_lon(o1[j], j) if j else o1[j] for j in (2, 1, 3, 0)]
    f2, *tied = lax.optimization_barrier((f2, *o1, *extra))
    o1, extra = tied[:LON], tied[LON:]
    m2 = model_call(1, t, f2, come)
    o2 = weight_call(1, t, m2, rows, own, extra)
    r2 = [to_lon(o2[j], j) if j else o2[j] for j in (2, 1, 3, 0)]
    return place_second(t, r2, place_first(t, r1, tile_rows))[None]


def solution(mesh):
    return jax.shard_map(
        shards,
        mesh=mesh,
        in_specs=(P("sub", None, "lat", "lon"), P(None, "lat", "lon"), P()),
        out_specs=P("sub", None, "lat", "lon"),
        check_vma=False,
    )
```
